256 devices in a mesh: row: 16 (over z_hi, y, core), col: 16 (over z_lo, x).
Axes of the slice: x: 4, y: 4, z: 8 (z_hi: 2, z_lo: 4; z = z_hi * 4 + z_lo), core: 2. Of those that a mesh axis runs over, the one named last changes fastest.
Arguments:
- features: float32 [131072, 256], P(('row', 'col')), may hold values from -6 to 6
- self_weight: float32 [256, 128], replicated, may hold values from -0.375 to 0.375
- neigh_weight: float32 [256, 128], replicated, may hold values from -0.75 to 0.75
- out_bias: float32 [128], replicated, may hold values from -3 to 3
- adjacency_tiles: int32 [1024, 32, 128, 128], P('row', 'col'), may hold values from 0 to 3, as said below
- tile_columns: int32 [1024, 32], P('row', 'col'), may hold values from 0 to 63
- live_counts: int32 [1024, 16], P('row', 'col'), may hold values from 1 to 2, as said below
- cotangent: float32 [131072, 128], P(('row', 'col')), may hold values from -6 to 6
Outputs:
- hidden_out: float32 [131072, 128], P(('row', 'col'))
- grad_features: float32 [131072, 256], P(('row', 'col'))
- grad_self: float32 [256, 128], replicated
- grad_neigh: float32 [256, 128], replicated
- grad_bias: float32 [128], replicated
The draws below stay inside these ranges and needn't reach their ends.
Inputs may be any that keep to these rules, and one draw needn't show every extreme that they name: `adjacency_tiles`: edge multiplicities; most entries are zero. `live_counts`: slots at or after this count in a tile-row's block are ignored, whatever they hold.
All inputs are finite; a program needn't handle non-finite values.
Results may differ from the reference program's by a relative error of at most 0.0003.
Values sent between devices are 32-bit elements; how exact they have to be, the bound alone decides.
A program may use at most 128 MiB of HBM per device.

```python
import jax
import jax.numpy as jnp
from jax import lax

NODES_DEV = 512
F_IN = 256
F_OUT = 128
TILE = 128
SLOTS = 2
KNN = 16
NODES = 131072
ROWS_BLK = 8192
COLS_BLK = 8192
TROWS = 64
TCOLS = 64
ALL_TROWS = 1024
GRID_COLS = 16
TILE_SLOTS = 32
N_ROW = 16
N_COL = 16


def draw_adjacency_tiles(key, part):
    full_shape = (ALL_TROWS, TILE_SLOTS, TILE, TILE)
    first_key, second_key = jax.random.split(jax.random.fold_in(key, 11))
    chance = jax.random.randint(first_key, full_shape, 0, TILE_SLOTS * TILE)
    multiple = jax.random.randint(second_key, full_shape, 1, 4)
    return jnp.where(chance < KNN, multiple, 0).astype(jnp.int32)


def draw_live_counts(key, part):
    full_shape = (ALL_TROWS, GRID_COLS)
    values = jax.random.randint(jax.random.fold_in(key, 23), full_shape, 1, SLOTS + 1)
    row_ids = lax.broadcasted_iota(jnp.int32, full_shape, 0)
    return jnp.where(row_ids == 0, SLOTS, values).astype(jnp.int32)


def set_ends(values, rng, smallest, high):
    place = [jax.random.randint(jax.random.fold_in(rng, axis), (), 0, length) for axis, length in enumerate(values.shape)]
    longest = values.shape.index(max(values.shape))
    next_to = place[:longest] + [(place[longest] + 1) % values.shape[longest]] + place[longest + 1:]
    return values.at[tuple(place)].set(smallest).at[tuple(next_to)].set(high)


def block_levels(key, shape, pieces, least, top_value):
    factor_of, own = 1.0, jax.random.fold_in(key, 6)
    for position, shards_of in pieces:
        draws = jnp.exp(jax.random.uniform(jax.random.fold_in(own, position), (shards_of,), jnp.float32, least / len(pieces), top_value / len(pieces)))
        factor_of = factor_of * jnp.repeat(draws, shape[position] // shards_of).reshape([-1 if axis == position else 1 for axis in range(len(shape))])
    return factor_of


def bell_draw(key, dims, scale, limit, pieces=(), kind=jnp.bfloat16):
    values = jax.random.normal(key, dims, jnp.float32) * scale
    if len(pieces) > 0:
        values = block_levels(key, dims, pieces, -0.22, 0.18) * values
    return jnp.clip(values, min=-limit, max=limit).astype(kind)


def setup_inputs(seed: int = 0) -> dict:
    splits = jax.random.split(jax.random.key(seed), 9)
    features = bell_draw(splits[0], (NODES, F_IN), 1.0, 6.0, ((0, 256),), jnp.float32)
    self_weight = bell_draw(splits[1], (F_IN, F_OUT), F_IN ** -0.5, 0.375, (), jnp.float32)
    neigh_weight = bell_draw(splits[2], (F_IN, F_OUT), (F_IN // 4) ** -0.5, 0.75, (), jnp.float32)
    out_bias = bell_draw(splits[3], (F_OUT,), 0.5, 3.0, (), jnp.float32)
    adjacency_tiles = draw_adjacency_tiles(jax.random.fold_in(splits[8], 71), 0)
    tile_columns = set_ends(jax.random.randint(splits[5], (ALL_TROWS, TILE_SLOTS), 0, TCOLS), jax.random.fold_in(splits[5], 1), 0, TCOLS - 1).astype(jnp.int32)
    live_counts = draw_live_counts(jax.random.fold_in(splits[8], 71), 0)
    cotangent = bell_draw(splits[7], (NODES, F_OUT), 1.0, 6.0, ((0, 256),), jnp.float32)
    return {"features": features, "self_weight": self_weight, "neigh_weight": neigh_weight, "out_bias": out_bias, "adjacency_tiles": adjacency_tiles, "tile_columns": tile_columns, "live_counts": live_counts, "cotangent": cotangent}


def live_weights(tile_values, count_block):
    slot_ids = jnp.arange(tile_values.shape[1], dtype=jnp.int32)
    live_slots = (slot_ids[None, :] < count_block).astype(jnp.float32)
    return tile_values.astype(jnp.float32) * live_slots[:, :, None, None]


def forward_tiles(weighted, column_block, source):
    tile_size = weighted.shape[2]
    feature_width = source.shape[1]
    source_tiles = source.reshape(-1, tile_size, feature_width)
    picked = source_tiles[column_block]
    products = jnp.einsum("tkab,tkbw->taw", weighted, picked, precision=lax.Precision.HIGHEST)
    return products.reshape(-1, feature_width)


def backward_tiles(weighted, column_block, source, col_tiles):
    tile_size = weighted.shape[2]
    feature_width = source.shape[1]
    source_tiles = source.reshape(-1, tile_size, feature_width)
    spread = jnp.einsum("tkab,taw->tkbw", weighted, source_tiles, precision=lax.Precision.HIGHEST)
    merged = jax.ops.segment_sum(spread.reshape(-1, tile_size, feature_width), column_block.reshape(-1), num_segments=col_tiles)
    return merged.reshape(-1, feature_width)


def reference(features, self_weight, neigh_weight, out_bias, adjacency_tiles, tile_columns, live_counts, cotangent):
    highest = lax.Precision.HIGHEST
    feature_grid = features.reshape(N_ROW, N_COL, NODES_DEV, F_IN)

    def device_tiles(row_id, col_id):
        row_start = (row_id * TROWS).astype(jnp.int32)
        col_start = (col_id * SLOTS).astype(jnp.int32)
        zero_start = jnp.zeros((), jnp.int32)
        tile_block = lax.dynamic_slice(adjacency_tiles, (row_start, col_start, zero_start, zero_start), (TROWS, SLOTS, TILE, TILE))
        column_block = lax.dynamic_slice(tile_columns, (row_start, col_start), (TROWS, SLOTS))
        count_block = lax.dynamic_slice(live_counts, (row_start, col_id.astype(jnp.int32)), (TROWS, 1))
        return live_weights(tile_block, count_block), column_block

    def forward_row(row_id):
        def step_col(carry, col_id):
            weighted, column_block = device_tiles(row_id, col_id)
            source = lax.dynamic_index_in_dim(feature_grid, col_id, 1, keepdims=False).reshape(COLS_BLK, F_IN)
            rows_total = carry[0] + forward_tiles(weighted, column_block, source)
            degree_total = carry[1] + jnp.sum(weighted, axis=(1, 3)).reshape(-1)
            return (rows_total, degree_total), None

        start = (jnp.zeros((ROWS_BLK, F_IN), jnp.float32), jnp.zeros((ROWS_BLK,), jnp.float32))
        result, ignored = lax.scan(step_col, start, jnp.arange(N_COL, dtype=jnp.int32))
        return result

    row_sums, degree_sums = lax.map(forward_row, jnp.arange(N_ROW, dtype=jnp.int32))
    degree = 1.0 + degree_sums.reshape(NODES)
    aggregated = row_sums.reshape(NODES, F_IN) / degree[:, None]
    pre_act = jnp.dot(features, self_weight, precision=highest) + jnp.dot(aggregated, neigh_weight, precision=highest) + out_bias
    hidden_out = jax.nn.silu(pre_act)
    sig_value = jax.nn.sigmoid(pre_act)
    grad_pre = cotangent * sig_value * (1.0 + pre_act * (1.0 - sig_value))
    scaled = grad_pre / degree[:, None]
    scaled_grid = scaled.reshape(N_ROW, ROWS_BLK, F_OUT)

    def backward_col(col_id):
        def step_row(carry, row_id):
            weighted, column_block = device_tiles(row_id, col_id)
            source = lax.dynamic_index_in_dim(scaled_grid, row_id, 0, keepdims=False)
            return carry + backward_tiles(weighted, column_block, source, TCOLS), None

        result, ignored = lax.scan(step_row, jnp.zeros((COLS_BLK, F_OUT), jnp.float32), jnp.arange(N_ROW, dtype=jnp.int32))
        return result

    back_cols = lax.map(backward_col, jnp.arange(N_COL, dtype=jnp.int32))
    back_rows = back_cols.reshape(N_COL, N_ROW, NODES_DEV, F_OUT).transpose(1, 0, 2, 3).reshape(NODES, F_OUT)
    grad_features = jnp.dot(grad_pre, self_weight.T, precision=highest) + jnp.dot(back_rows, neigh_weight.T, precision=highest)
    factor = 1.0 / (NODES ** 0.5)
    grad_self = jnp.dot(features.T, grad_pre, precision=highest) * factor
    grad_neigh = jnp.dot(aggregated.T, grad_pre, precision=highest) * factor
    grad_bias = jnp.sum(grad_pre, axis=0) * factor
    return (hidden_out, grad_features, grad_self, grad_neigh, grad_bias)
```

```python
import math

import jax
import jax.numpy as jnp
from jax import lax
from jax.experimental import pallas as pl
from jax.experimental.pallas import tpu as pltpu
from jax.sharding import PartitionSpec as P

MESH = pl.DeviceIdType.MESH
F32 = jnp.float32
BF16 = jnp.bfloat16
HIGHEST = lax.Precision.HIGHEST

BLK = 512
HALF = BLK // 2
TILE = 128
TPB = BLK // TILE
GRID = 16
TROWS = TPB * GRID
DEG = 8
PACK = 24
PIECE = 16


class Place:
    def __init__(self):
        row, col = lax.axis_index("row"), lax.axis_index("col")
        self.row, self.col = row, col
        self.core = lax.rem(row, 2)
        self.y = lax.rem(lax.div(row, 2), 4)
        self.zh = lax.div(row, 8)
        self.x = lax.rem(col, 4)
        self.zl = lax.div(col, 4)
        self.z = self.zh * 4 + self.zl

    def at(self, core=None, y=None, z=None, x=None):
        core = self.core if core is None else core
        y = self.y if y is None else y
        z = self.z if z is None else z
        x = self.x if x is None else x
        return (lax.div(z, 4) * 4 + y) * 2 + core, lax.rem(z, 4) * 4 + x

    def partner(self):
        return self.at(core=1 - self.core)

    def ys(self, step):
        return lax.rem(self.y + step, 4)

    def xs(self, step):
        return lax.rem(self.x + step, 4)

    def zs(self, step):
        return lax.rem(self.z + step, 8)

    def zline(self, step):
        return lax.rem(self.zl + step, 4)


class Wire:
    def __init__(self, send, recv):
        self.send, self.recv, self.copies = send, recv, []

    def go(self, src, dst, device):
        i = len(self.copies)
        copy = pltpu.make_async_remote_copy(
            src_ref=src,
            dst_ref=dst,
            send_sem=self.send.at[i],
            recv_sem=self.recv.at[i],
            device_id=device,
            device_id_type=MESH,
        )
        copy.start()
        self.copies.append(copy)
        return copy

    def drain(self):
        for copy in self.copies:
            copy.wait_send()


def greet(peers):
    barrier = pltpu.get_barrier_semaphore()
    for peer in peers:
        pl.semaphore_signal(barrier, inc=1, device_id=peer, device_id_type=MESH)
    return barrier


def split(value):
    high = value.astype(BF16)
    low = (value - high.astype(F32)).astype(BF16)
    return jnp.concatenate([high, low], axis=1)


def dot_f32(a, b, dims):
    return lax.dot_general(a, b, (dims, ((), ())), precision=HIGHEST, preferred_element_type=F32)


FWD_COPIES = 21 + 19 + 19


def forward_kernel(
    cols_ref, live_ref, feat_ref, ws_ref, wn_ref, bias_ref, cot_ref, adj_ref,
    hid_ref, gp_ref, sall_ref, adjt_ref, gself_ref, gbias_ref,
    hall, adjb, part, xl1, xr1, xl2, xr2, zin, zrel, selfp, stage, stage_sem, send, recv,
):
    me = Place()
    wire = Wire(send, recv)
    right, left = me.at(x=me.xs(1)), me.at(x=me.xs(3))
    up, down = me.at(y=me.ys(1)), me.at(y=me.ys(3))
    far, near = me.at(z=me.zs(2)), me.at(z=me.zs(6))
    line = {d: me.at(z=me.zh * 4 + me.zline(d)) for d in (1, 2, 3)}
    peers = [me.partner(), up, down, right, left, far, near, line[1], line[2], line[3]]
    barrier = greet(peers)

    def fetch(chunk, slot):
        return pltpu.make_async_copy(adj_ref.at[pl.ds(chunk * TPB, TPB)], stage.at[slot], stage_sem.at[slot])

    fetch(0, 0).start()
    fetch(1, 1).start()

    def block(row):
        return hall.at[pl.ds(row * TPB, TPB)]

    def block_half(row, half):
        return hall.at[pl.ds(row * TPB + half * (TPB // 2), TPB // 2)]

    def row_of(y, zh, core):
        return (zh * 4 + y) * 2 + core

    own = dot_f32(feat_ref[...], wn_ref[...], ((1,), (0,)))
    hall[pl.ds(me.row * TPB, TPB)] = own.reshape(TPB, TILE, TILE)
    pl.semaphore_wait(barrier, len(peers))

    partner = me.partner()

    def mine(y, zh):
        return row_of(y, zh, me.core)

    def share(y, zh):
        return wire.go(block(mine(y, zh)), block(mine(y, zh)), partner)

    z_up = wire.go(block_half(me.row, 0), zrel.at[0], far)
    z_down = wire.go(block_half(me.row, 1), zrel.at[1], near)
    y_up = wire.go(block(me.row), block(me.row), up)
    y_down = wire.go(block(me.row), block(me.row), down)
    shared = [share(me.y, me.zh)]

    def convert(chunk, carry):
        slot = lax.rem(chunk, 2)
        fetch(chunk, slot).wait()
        degrees = []
        for i in range(TPB):
            t = chunk * TPB + i
            live = live_ref[t, 0]
            tiles = [jnp.where(live > k, stage[slot, i, k].astype(F32), 0.0) for k in range(2)]
            turned = [tile.T for tile in tiles]
            degrees.append(jnp.sum(turned[0] + turned[1], axis=0, keepdims=True))
            adjb[t] = jnp.concatenate(tiles, axis=1).astype(BF16)
            adjt_ref[t] = jnp.concatenate(turned, axis=0).astype(BF16)
        part[chunk, BLK:, :] = jnp.concatenate(degrees + [jnp.zeros((DEG - TPB, TILE), F32)], axis=0)

        @pl.when(chunk + 2 < GRID)
        def _():
            fetch(chunk + 2, slot).start()

        return carry

    lax.fori_loop(0, 4, convert, 0)
    z_up.wait_recv()
    source = mine(me.y, lax.div(me.zs(6), 4))
    zf_up = wire.go(zrel.at[0], block_half(source, 0), far)
    z_down.wait_recv()
    source = mine(me.y, lax.div(me.zs(2), 4))
    zf_down = wire.go(zrel.at[1], block_half(source, 1), near)
    lax.fori_loop(4, 7, convert, 0)

    def relay(zh, first, second):
        first.wait_recv()
        row = mine(me.ys(3), zh)
        one = wire.go(block_half(row, 0), block_half(row, 0), up)
        shared.append(share(me.ys(3), zh))
        second.wait_recv()
        row = mine(me.ys(1), zh)
        two = wire.go(block_half(row, 1), block_half(row, 1), down)
        shared.append(share(me.ys(1), zh))
        return one, two

    relays = relay(me.zh, y_up, y_down)
    lax.fori_loop(7, 11, convert, 0)
    other = 1 - me.zh
    zf_up.wait_recv()
    zf_down.wait_recv()
    row = mine(me.y, other)
    y_up = wire.go(block(row), block(row), up)
    y_down = wire.go(block(row), block(row), down)
    shared.append(share(me.y, other))
    relays[0].wait_recv()
    relays[1].wait_recv()
    shared.append(share(me.ys(2), me.zh))
    lax.fori_loop(11, GRID, convert, 0)
    relays = relay(other, y_up, y_down)
    selfp[...] = dot_f32(feat_ref[...], ws_ref[...], ((1,), (0,)))
    relays[0].wait_recv()
    relays[1].wait_recv()
    shared.append(share(me.ys(2), other))
    for copy in shared:
        copy.wait_recv()

    def multiply(zl, x):
        shard = zl * 4 + x

        def tile_row(i, carry):
            t = shard * TPB + i
            picked = jnp.concatenate([hall[cols_ref[t, 0]], hall[cols_ref[t, 1]]], axis=0)
            both = jnp.dot(adjb[t], split(picked), preferred_element_type=F32)
            part[shard, pl.ds(pl.multiple_of(i * TILE, TILE), TILE), :] = both[:, :TILE] + both[:, TILE:]
            return carry

        lax.fori_loop(0, TPB, tile_row, 0)
        return shard

    order = (2, 1, 3, 0)
    low, high = pl.ds(0, HALF), pl.ds(HALF, HALF + DEG)
    firsts = []
    for d in order:
        shard = multiply(me.zline(d), me.xs(2))
        firsts.append(
            (
                wire.go(part.at[shard, low], xl1.at[d], right),
                wire.go(part.at[shard, high], xr1.at[d], left),
            )
        )
    seconds = []
    for d, (from_left, from_right) in zip(order, firsts):
        shard = multiply(me.zline(d), me.xs(1))
        from_left.wait_recv()
        part[shard, low, :] += xl1[d]
        one = wire.go(part.at[shard], xl2.at[d], right)
        shard = multiply(me.zline(d), me.xs(3))
        from_right.wait_recv()
        part[shard, high, :] += xr1[d]
        two = wire.go(part.at[shard], xr2.at[d], left)
        seconds.append((one, two))
    for d in order:
        multiply(me.zline(d), me.x)
    arrivals = []
    for d, (from_left, from_right) in zip(order, seconds):
        shard = me.zline(d) * 4 + me.x
        from_left.wait_recv()
        from_right.wait_recv()
        part[shard] += xl2[d] + xr2[d]
        if d:
            arrivals.append(wire.go(part.at[shard], zin.at[d - 1], line[d]))
    for copy in arrivals:
        copy.wait_recv()
    total = part[me.col] + zin[0] + zin[1] + zin[2]

    for i in range(TPB):
        rows = pl.ds(i * TILE, TILE)
        counts = jnp.broadcast_to(total[BLK + i : BLK + i + 1, :], (TILE, TILE)).T
        degree = 1.0 + counts
        pre = selfp[rows, :] + total[i * TILE : (i + 1) * TILE, :] / degree + bias_ref[...]
        sig = jax.nn.sigmoid(pre)
        hid_ref[rows, :] = pre * sig
        grad = cot_ref[rows, :] * sig * (1.0 + pre * (1.0 - sig))
        gp_ref[rows, :] = grad
        sall_ref[me.col, rows, :] = grad / degree

    def spread(block_col):
        return (
            wire.go(sall_ref.at[block_col], sall_ref.at[block_col], right),
            wire.go(sall_ref.at[block_col], sall_ref.at[block_col], left),
        )

    def pass_on(zl, pair):
        pair[0].wait_recv()
        from_left = zl * 4 + me.xs(3)
        one = wire.go(sall_ref.at[from_left, pl.ds(0, HALF)], sall_ref.at[from_left, pl.ds(0, HALF)], right)
        pair[1].wait_recv()
        from_right = zl * 4 + me.xs(1)
        two = wire.go(sall_ref.at[from_right, pl.ds(HALF, HALF)], sall_ref.at[from_right, pl.ds(HALF, HALF)], left)
        return one, two

    sent = {d: wire.go(sall_ref.at[me.col], sall_ref.at[me.col], line[d]) for d in (1, 3, 2)}
    pending = [(me.zl, spread(me.col))]
    gself_ref[...] = dot_f32(feat_ref[...], gp_ref[...], ((0,), (0,)))
    gbias_ref[...] = jnp.sum(gp_ref[...], axis=0, keepdims=True)
    last = []
    for d in (1, 3, 2):
        zl = me.zline(4 - d)
        sent[d].wait_recv()
        pending.append((zl, spread(zl * 4 + me.x)))
        last += pass_on(*pending.pop(0))
    last += pass_on(*pending.pop(0))
    for copy in last:
        copy.wait_recv()
    wire.drain()


def backward_kernel(cols_ref, adjt_ref, scaled_ref, back_ref):
    step = pl.program_id(0)

    @pl.when(step == 0)
    def _():
        back_ref[...] = jnp.zeros_like(back_ref)

    rows = scaled_ref.shape[0]

    def tile_row(i, carry):
        t = step * rows + i
        both = jnp.dot(adjt_ref[i], split(scaled_ref[i]), preferred_element_type=F32)
        both = both[:, :TILE] + both[:, TILE:]
        back_ref[cols_ref[t, 0]] += both[:TILE]
        back_ref[cols_ref[t, 1]] += both[TILE:]
        return carry

    lax.fori_loop(0, rows, tile_row, 0)


BACK_COPIES = 8 + 8 + 4 + 1 + 3 + 3 + 7 + 3 + 3 + 1


def return_kernel(
    factor, back_ref, feat_ref, gp_ref, ws_ref, wn_ref, gself_ref, gbias_ref,
    gf_ref, gs_ref, gn_ref, gb_ref,
    sums, rc, yl1, yr1, yl2, yr2, zin, zrel, pack, r1, r2, r3, r4, full, load_sem, send, recv,
):
    me = Place()
    wire = Wire(send, recv)
    up, down = me.at(y=me.ys(1)), me.at(y=me.ys(3))
    far, near = me.at(z=me.zs(2)), me.at(z=me.zs(6))
    partner = me.partner()
    peers = [partner]
    peers += [me.at(y=me.ys(d)) for d in (1, 2, 3)]
    peers += [me.at(x=me.xs(d)) for d in (1, 2, 3)]
    peers += [me.at(z=me.zs(d)) for d in range(1, 8)]
    barrier = greet(peers)
    other = 1 - me.zh
    order = [(other, 2), (me.zh, 2), (other, 1), (other, 3), (me.zh, 1), (me.zh, 3), (other, 0), (me.zh, 0)]

    def group(zh, d):
        return zh * 4 + me.ys(d)

    gf_ref[...] = dot_f32(gp_ref[...], ws_ref[...], ((1,), (1,)))
    pl.semaphore_wait(barrier, len(peers))

    from_core = {}
    for n, (zh, d) in enumerate(order):
        g = group(zh, d)
        from_core[n] = wire.go(back_ref.at[g, 1 - me.core], rc.at[g], partner)

    def summed(n):
        zh, d = order[n]
        g = group(zh, d)
        from_core[n].wait_recv()
        sums[g] = back_ref[g, me.core] + rc[g]
        return g

    low, high = pl.ds(0, HALF), pl.ds(HALF, HALF)
    firsts = []
    for n in (0, 1):
        g = summed(n)
        firsts.append((wire.go(sums.at[g, low], yl1.at[n], up), wire.go(sums.at[g, high], yr1.at[n], down)))
    seconds = []
    for n in (0, 1):
        g = summed(2 + 2 * n)
        firsts[n][0].wait_recv()
        sums[g, low, :] += yl1[n]
        one = wire.go(sums.at[g], yl2.at[n], up)
        g = summed(3 + 2 * n)
        firsts[n][1].wait_recv()
        sums[g, high, :] += yr1[n]
        two = wire.go(sums.at[g], yr2.at[n], down)
        seconds.append((one, two))

    def finished(n):
        g = summed(6 + n)
        seconds[n][0].wait_recv()
        seconds[n][1].wait_recv()
        sums[g] += yl2[n] + yr2[n]
        return g

    g = finished(0)
    z_up = wire.go(sums.at[g, low], zrel.at[0], far)
    z_down = wire.go(sums.at[g, high], zrel.at[1], near)
    z_up.wait_recv()
    zf_up = wire.go(zrel.at[0], zin.at[low], far)
    z_down.wait_recv()
    zf_down = wire.go(zrel.at[1], zin.at[high], near)
    g = finished(1)
    zf_up.wait_recv()
    zf_down.wait_recv()
    back_rows = sums[g] + zin[...]

    gneigh = dot_f32(feat_ref[...], back_rows, ((0,), (0,)))
    for core in range(2):
        source = gself_ref[...] if core == 0 else gneigh
        for n in range(16):
            pack[core, n // 4, n % 4, pl.ds(0, PIECE), :] = source[n * PIECE : (n + 1) * PIECE, :]
            pack[core, n // 4, n % 4, pl.ds(PIECE, PACK - PIECE), :] = jnp.zeros((PACK - PIECE, TILE), F32)
    pack[0, 0, 0, pl.ds(PIECE, 1), :] = gbias_ref[...]

    copy = wire.go(pack.at[1 - me.core], r1, partner)
    gf_ref[...] += dot_f32(back_rows, wn_ref[...], ((1,), (1,)))
    copy.wait_recv()
    pack[me.core] += r1[...]
    copies = [wire.go(pack.at[me.core, me.xs(d)], r2.at[d - 1], me.at(x=me.xs(d))) for d in (2, 1, 3)]
    for copy in copies:
        copy.wait_recv()
    pack[me.core, me.x] += r2[0] + r2[1] + r2[2]
    copies = [wire.go(pack.at[me.core, me.x, me.ys(d)], r3.at[d - 1], me.at(y=me.ys(d))) for d in (2, 1, 3)]
    for copy in copies:
        copy.wait_recv()
    r4[me.z] = pack[me.core, me.x, me.y] + r3[0] + r3[1] + r3[2]
    copies = [wire.go(r4.at[me.z], r4.at[me.z], me.at(z=me.zs(d))) for d in (4, 3, 5, 2, 6, 1, 7)]
    for copy in copies:
        copy.wait_recv()
    total = r4[0]
    for n in range(1, 8):
        total = total + r4[n]
    full[me.core, me.x, me.y] = total
    view = full.at[me.core, me.x, me.y]
    copies = [wire.go(view, view, me.at(y=me.ys(d))) for d in (2, 1, 3)]
    for copy in copies:
        copy.wait_recv()
    view = full.at[me.core, me.x]
    copies = [wire.go(view, view, me.at(x=me.xs(d))) for d in (2, 1, 3)]
    for copy in copies:
        copy.wait_recv()
    view = full.at[me.core]
    wire.go(view, view, partner).wait_recv()
    for core, out in ((0, gs_ref), (1, gn_ref)):
        for n in range(16):
            out[pl.ds(n * PIECE, PIECE), :] = full[core, n // 4, n % 4, pl.ds(0, PIECE), :] * factor
    gb_ref[...] = full[0, 0, 0, pl.ds(PIECE, 1), :] * factor
    wire.drain()


def local(features, self_weight, neigh_weight, out_bias, adjacency_tiles, tile_columns, live_counts, cotangent):
    vmem = pl.BlockSpec(memory_space=pltpu.VMEM)
    smem = pl.BlockSpec(memory_space=pltpu.SMEM)
    hbm = pl.BlockSpec(memory_space=pl.ANY)
    fin, fout = self_weight.shape

    def shape(*dims, dtype=F32):
        return jax.ShapeDtypeStruct(dims, dtype)

    dma = pltpu.SemaphoreType.DMA
    hidden, grad_pre, scaled, adjt, gself, gbias = pl.pallas_call(
        forward_kernel,
        out_shape=[
            shape(BLK, fout),
            shape(BLK, fout),
            shape(GRID, BLK, fout),
            shape(TROWS, 2 * TILE, TILE, dtype=BF16),
            shape(fin, fout),
            shape(1, fout),
        ],
        in_specs=[smem, smem] + [vmem] * 5 + [hbm],
        out_specs=[vmem] * 6,
        scratch_shapes=[
            pltpu.VMEM((TROWS, TILE, fout), F32),
            pltpu.VMEM((TROWS, TILE, 2 * TILE), BF16),
            pltpu.VMEM((GRID, BLK + DEG, fout), F32),
            pltpu.VMEM((4, HALF, fout), F32),
            pltpu.VMEM((4, HALF + DEG, fout), F32),
            pltpu.VMEM((4, BLK + DEG, fout), F32),
            pltpu.VMEM((4, BLK + DEG, fout), F32),
            pltpu.VMEM((3, BLK + DEG, fout), F32),
            pltpu.VMEM((2, TPB // 2, TILE, fout), F32),
            pltpu.VMEM((BLK, fout), F32),
            pltpu.VMEM((2, TPB, 2, TILE, TILE), jnp.int32),
            dma((2,)),
            dma((FWD_COPIES,)),
            dma((FWD_COPIES,)),
        ],
        compiler_params=pltpu.CompilerParams(collective_id=0, has_side_effects=True, vmem_limit_bytes=48 << 20),
        name="forward",
    )(tile_columns, live_counts, features, self_weight, neigh_weight, out_bias.reshape(1, fout), cotangent, adjacency_tiles)

    steps = 8
    rows = TROWS // steps
    back = pl.pallas_call(
        backward_kernel,
        grid=(steps,),
        out_shape=shape(TROWS, TILE, fout),
        in_specs=[
            smem,
            pl.BlockSpec((rows, 2 * TILE, TILE), lambda i: (i, 0, 0)),
            pl.BlockSpec((rows, TILE, fout), lambda i: (i, 0, 0)),
        ],
        out_specs=pl.BlockSpec((TROWS, TILE, fout), lambda i: (0, 0, 0)),
        compiler_params=pltpu.CompilerParams(vmem_limit_bytes=32 << 20),
        name="backward",
    )(tile_columns, adjt, scaled.reshape(TROWS, TILE, fout))

    nodes = BLK * lax.axis_size("row") * lax.axis_size("col")
    factor = 1.0 / math.sqrt(nodes)
    grad_features, grad_self, grad_neigh, grad_bias = pl.pallas_call(
        lambda *refs: return_kernel(factor, *refs),
        out_shape=[shape(BLK, fin), shape(fin, fout), shape(fin, fout), shape(1, fout)],
        in_specs=[vmem] * 7,
        out_specs=[vmem] * 4,
        scratch_shapes=[
            pltpu.VMEM((8, BLK, fout), F32),
            pltpu.VMEM((8, BLK, fout), F32),
            pltpu.VMEM((2, HALF, fout), F32),
            pltpu.VMEM((2, HALF, fout), F32),
            pltpu.VMEM((2, BLK, fout), F32),
            pltpu.VMEM((2, BLK, fout), F32),
            pltpu.VMEM((BLK, fout), F32),
            pltpu.VMEM((2, HALF, fout), F32),
            pltpu.VMEM((2, 4, 4, PACK, fout), F32),
            pltpu.VMEM((4, 4, PACK, fout), F32),
            pltpu.VMEM((3, 4, PACK, fout), F32),
            pltpu.VMEM((3, PACK, fout), F32),
            pltpu.VMEM((8, PACK, fout), F32),
            pltpu.VMEM((2, 4, 4, PACK, fout), F32),
            dma((1,)),
            dma((BACK_COPIES,)),
            dma((BACK_COPIES,)),
        ],
        compiler_params=pltpu.CompilerParams(collective_id=1, has_side_effects=True, vmem_limit_bytes=48 << 20),
        name="backward_return",
    )(back.reshape(8, 2, BLK, fout), features, grad_pre, self_weight, neigh_weight, gself, gbias)
    return hidden, grad_features, grad_self, grad_neigh, grad_bias.reshape(fout)


def solution(mesh):
    return jax.shard_map(
        local,
        mesh=mesh,
        in_specs=(
            P(("row", "col"), None),
            P(),
            P(),
            P(),
            P("row", "col", None, None),
            P("row", "col"),
            P("row", "col"),
            P(("row", "col"), None),
        ),
        out_specs=(P(("row", "col"), None), P(("row", "col"), None), P(), P(), P()),
        check_vma=False,
    )
```

```python
import math

import jax
import jax.numpy as jnp
from jax import lax
from jax.experimental import pallas as pl
from jax.experimental.pallas import tpu as pltpu
from jax.sharding import PartitionSpec as P

MESH = pl.DeviceIdType.MESH
F32 = jnp.float32
BF16 = jnp.bfloat16
HIGHEST = lax.Precision.HIGHEST

BLK = 512
HALF = BLK // 2
TILE = 128
TPB = BLK // TILE
GRID = 16
TROWS = TPB * GRID
DEG = 8


class Place:
    def __init__(self):
        row, col = lax.axis_index("row"), lax.axis_index("col")
        self.row, self.col = row, col
        self.core = lax.rem(row, 2)
        self.y = lax.rem(lax.div(row, 2), 4)
        self.zh = lax.div(row, 8)
        self.x = lax.rem(col, 4)
        self.zl = lax.div(col, 4)
        self.z = self.zh * 4 + self.zl

    def at(self, core=None, y=None, z=None, x=None):
        core = self.core if core is None else core
        y = self.y if y is None else y
        z = self.z if z is None else z
        x = self.x if x is None else x
        return (lax.div(z, 4) * 4 + y) * 2 + core, lax.rem(z, 4) * 4 + x

    def partner(self):
        return self.at(core=1 - self.core)

    def ys(self, step):
        return lax.rem(self.y + step, 4)

    def xs(self, step):
        return lax.rem(self.x + step, 4)

    def zs(self, step):
        return lax.rem(self.z + step, 8)

    def zline(self, step):
        return lax.rem(self.zl + step, 4)


class Wire:
    def __init__(self, send, recv):
        self.send, self.recv, self.copies = send, recv, []

    def go(self, src, dst, device):
        i = len(self.copies)
        copy = pltpu.make_async_remote_copy(
            src_ref=src,
            dst_ref=dst,
            send_sem=self.send.at[i],
            recv_sem=self.recv.at[i],
            device_id=device,
            device_id_type=MESH,
        )
        copy.start()
        self.copies.append(copy)
        return copy

    def drain(self):
        for copy in self.copies:
            copy.wait_send()


def greet(peers):
    barrier = pltpu.get_barrier_semaphore()
    for peer in peers:
        pl.semaphore_signal(barrier, inc=1, device_id=peer, device_id_type=MESH)
    return barrier


def split(value):
    high = value.astype(BF16)
    low = (value - high.astype(F32)).astype(BF16)
    return jnp.concatenate([high, low], axis=1)


def dot_f32(a, b, dims):
    return lax.dot_general(a, b, (dims, ((), ())), precision=HIGHEST, preferred_element_type=F32)


FWD_COPIES = 21 + 19 + 19


def forward_kernel(
    cols_hbm, live_hbm, feat_hbm, ws_hbm, wn_hbm, bias_hbm, cot_hbm, adj_ref,
    hid_ref, gp_ref, sall_ref, adjt_ref, gself_ref, gbias_ref, feat_out, ws_out, wn_out,
    hall, adjb, part, xl1, xr1, xl2, xr2, zin, zrel, selfp, stage, bias_ref, cot_ref, cols_ref, live_ref, stage_sem, load_sem, send, recv,
):
    feat_ref, ws_ref, wn_ref = feat_out, ws_out, wn_out
    pairs = ((feat_hbm, feat_ref), (wn_hbm, wn_ref), (ws_hbm, ws_ref), (bias_hbm, bias_ref), (cot_hbm, cot_ref))
    pairs += ((live_hbm, live_ref), (cols_hbm, cols_ref))
    loads = [pltpu.make_async_copy(a, b, load_sem.at[i]) for i, (a, b) in enumerate(pairs)]
    for load in loads:
        load.start()
    me = Place()
    wire = Wire(send, recv)
    right, left = me.at(x=me.xs(1)), me.at(x=me.xs(3))
    up, down = me.at(y=me.ys(1)), me.at(y=me.ys(3))
    far, near = me.at(z=me.zs(2)), me.at(z=me.zs(6))
    line = {d: me.at(z=me.zh * 4 + me.zline(d)) for d in (1, 2, 3)}
    peers = [me.partner(), up, down, right, left, far, near, line[1], line[2], line[3]]
    barrier = greet(peers)

    def fetch(chunk, slot):
        return pltpu.make_async_copy(adj_ref.at[pl.ds(chunk * TPB, TPB)], stage.at[slot], stage_sem.at[slot])

    fetch(0, 0).start()
    fetch(1, 1).start()

    def block(row):
        return hall.at[pl.ds(row * TPB, TPB)]

    def block_half(row, half):
        return hall.at[pl.ds(row * TPB + half * (TPB // 2), TPB // 2)]

    def row_of(y, zh, core):
        return (zh * 4 + y) * 2 + core

    loads[0].wait()
    loads[1].wait()
    own = dot_f32(feat_ref[...], wn_ref[...], ((1,), (0,)))
    hall[pl.ds(me.row * TPB, TPB)] = own.reshape(TPB, TILE, TILE)
    pl.semaphore_wait(barrier, len(peers))

    partner = me.partner()

    def mine(y, zh):
        return row_of(y, zh, me.core)

    def share(y, zh):
        return wire.go(block(mine(y, zh)), block(mine(y, zh)), partner)

    z_up = wire.go(block_half(me.row, 0), zrel.at[0], far)
    z_down = wire.go(block_half(me.row, 1), zrel.at[1], near)
    y_up = wire.go(block(me.row), block(me.row), up)
    y_down = wire.go(block(me.row), block(me.row), down)
    shared = [share(me.y, me.zh)]

    def convert(chunk, carry):
        slot = lax.rem(chunk, 2)
        fetch(chunk, slot).wait()
        degrees = []
        for i in range(TPB):
            t = chunk * TPB + i
            live = live_ref[0, t]
            tiles = [jnp.where(live > k, stage[slot, i, k].astype(F32), 0.0) for k in range(2)]
            turned = [tile.T for tile in tiles]
            degrees.append(jnp.sum(turned[0] + turned[1], axis=0, keepdims=True))
            adjb[t] = jnp.concatenate(tiles, axis=1).astype(BF16)
            adjt_ref[t] = jnp.concatenate(turned, axis=0).astype(BF16)
        part[chunk, BLK:, :] = jnp.concatenate(degrees + [jnp.zeros((DEG - TPB, TILE), F32)], axis=0)

        @pl.when(chunk + 2 < GRID)
        def _():
            fetch(chunk + 2, slot).start()

        return carry

    for load in loads[2:]:
        load.wait()
    lax.fori_loop(0, 4, convert, 0)
    z_up.wait_recv()
    source = mine(me.y, lax.div(me.zs(6), 4))
    zf_up = wire.go(zrel.at[0], block_half(source, 0), far)
    z_down.wait_recv()
    source = mine(me.y, lax.div(me.zs(2), 4))
    zf_down = wire.go(zrel.at[1], block_half(source, 1), near)
    lax.fori_loop(4, 7, convert, 0)

    def relay(zh, first, second):
        first.wait_recv()
        row = mine(me.ys(3), zh)
        one = wire.go(block_half(row, 0), block_half(row, 0), up)
        shared.append(share(me.ys(3), zh))
        second.wait_recv()
        row = mine(me.ys(1), zh)
        two = wire.go(block_half(row, 1), block_half(row, 1), down)
        shared.append(share(me.ys(1), zh))
        return one, two

    relays = relay(me.zh, y_up, y_down)
    lax.fori_loop(7, 11, convert, 0)
    other = 1 - me.zh
    zf_up.wait_recv()
    zf_down.wait_recv()
    row = mine(me.y, other)
    y_up = wire.go(block(row), block(row), up)
    y_down = wire.go(block(row), block(row), down)
    shared.append(share(me.y, other))
    relays[0].wait_recv()
    relays[1].wait_recv()
    shared.append(share(me.ys(2), me.zh))
    lax.fori_loop(11, GRID, convert, 0)
    relays = relay(other, y_up, y_down)
    selfp[...] = dot_f32(feat_ref[...], ws_ref[...], ((1,), (0,)))
    relays[0].wait_recv()
    relays[1].wait_recv()
    shared.append(share(me.ys(2), other))
    for copy in shared:
        copy.wait_recv()

    def multiply(zl, x):
        shard = zl * 4 + x

        def tile_row(i, carry):
            t = shard * TPB + i
            picked = jnp.concatenate([hall[cols_ref[0, t]], hall[cols_ref[1, t]]], axis=0)
            both = jnp.dot(adjb[t], split(picked), preferred_element_type=F32)
            part[shard, pl.ds(pl.multiple_of(i * TILE, TILE), TILE), :] = both[:, :TILE] + both[:, TILE:]
            return carry

        lax.fori_loop(0, TPB, tile_row, 0)
        return shard

    order = (2, 1, 3, 0)
    low, high = pl.ds(0, HALF), pl.ds(HALF, HALF + DEG)
    firsts = []
    for d in order:
        shard = multiply(me.zline(d), me.xs(2))
        firsts.append(
            (
                wire.go(part.at[shard, low], xl1.at[d], right),
                wire.go(part.at[shard, high], xr1.at[d], left),
            )
        )
    seconds = []
    for d, (from_left, from_right) in zip(order, firsts):
        shard = multiply(me.zline(d), me.xs(1))
        from_left.wait_recv()
        part[shard, low, :] += xl1[d]
        one = wire.go(part.at[shard], xl2.at[d], right)
        shard = multiply(me.zline(d), me.xs(3))
        from_right.wait_recv()
        part[shard, high, :] += xr1[d]
        two = wire.go(part.at[shard], xr2.at[d], left)
        seconds.append((one, two))
    for d in order:
        multiply(me.zline(d), me.x)
    arrivals = []
    for d, (from_left, from_right) in zip(order, seconds):
        shard = me.zline(d) * 4 + me.x
        from_left.wait_recv()
        from_right.wait_recv()
        part[shard] += xl2[d] + xr2[d]
        if d:
            arrivals.append(wire.go(part.at[shard], zin.at[d - 1], line[d]))
    for copy in arrivals:
        copy.wait_recv()
    total = part[me.col] + zin[0] + zin[1] + zin[2]

    for i in range(TPB):
        rows = pl.ds(i * TILE, TILE)
        counts = jnp.broadcast_to(total[BLK + i : BLK + i + 1, :], (TILE, TILE)).T
        degree = 1.0 + counts
        pre = selfp[rows, :] + total[i * TILE : (i + 1) * TILE, :] / degree + bias_ref[...]
        sig = jax.nn.sigmoid(pre)
        hid_ref[rows, :] = pre * sig
        grad = cot_ref[rows, :] * sig * (1.0 + pre * (1.0 - sig))
        gp_ref[rows, :] = grad
        sall_ref[me.col, rows, :] = grad / degree

    def spread(block_col):
        return (
            wire.go(sall_ref.at[block_col], sall_ref.at[block_col], right),
            wire.go(sall_ref.at[block_col], sall_ref.at[block_col], left),
        )

    def pass_on(zl, pair):
        pair[0].wait_recv()
        from_left = zl * 4 + me.xs(3)
        one = wire.go(sall_ref.at[from_left, pl.ds(0, HALF)], sall_ref.at[from_left, pl.ds(0, HALF)], right)
        pair[1].wait_recv()
        from_right = zl * 4 + me.xs(1)
        two = wire.go(sall_ref.at[from_right, pl.ds(HALF, HALF)], sall_ref.at[from_right, pl.ds(HALF, HALF)], left)
        return one, two

    sent = {d: wire.go(sall_ref.at[me.col], sall_ref.at[me.col], line[d]) for d in (1, 3, 2)}
    pending = [(me.zl, spread(me.col))]
    gself_ref[...] = dot_f32(feat_ref[...], gp_ref[...], ((0,), (0,)))
    gbias_ref[...] = jnp.sum(gp_ref[...], axis=0, keepdims=True)
    last = []
    for d in (1, 3, 2):
        zl = me.zline(4 - d)
        sent[d].wait_recv()
        pending.append((zl, spread(zl * 4 + me.x)))
        last += pass_on(*pending.pop(0))
    last += pass_on(*pending.pop(0))
    for copy in last:
        copy.wait_recv()
    wire.drain()


def backward_kernel(cols_ref, adjt_ref, scaled_ref, hid_ref, back_ref, hid_out, hid_sem):
    step = pl.program_id(0)
    rows = scaled_ref.shape[0]
    hidden = pltpu.make_async_copy(hid_ref, hid_out, hid_sem.at[0])

    @pl.when(step == 0)
    def _():
        hidden.start()
        back_ref[...] = jnp.zeros_like(back_ref)

    for start in range(0, rows, 4):
        parts = []
        for i in range(start, start + 4):
            both = jnp.dot(adjt_ref[i], split(scaled_ref[i]), preferred_element_type=F32)
            parts.append(both[:, :TILE] + both[:, TILE:])
        for i in range(start, start + 4):
            t = step * rows + i
            back_ref[cols_ref[0, t]] += parts[i - start][:TILE]
            back_ref[cols_ref[1, t]] += parts[i - start][TILE:]

    @pl.when(step == pl.num_programs(0) - 1)
    def _():
        hidden.wait()


SUM_COPIES = 7 + 3 + 7 + 3 + 7
BACK_COPIES = 8 + 8 + 4 + 2 * SUM_COPIES


def others(me):
    return [(me.core, me.xs(2)), (1 - me.core, me.xs(2))] + [
        (me.core, me.xs(1)), (1 - me.core, me.xs(1)), (me.core, me.xs(3)), (1 - me.core, me.xs(3)), (1 - me.core, me.x)
    ]


def pack_rows(pack, rows):
    for n in range(32):
        pack[n // 16, n // 4 % 4, n % 4, pl.ds(0, 8), :] = rows[n * 8 : (n + 1) * 8, :]


def total_over_all(me, wire, pack, r1, r2, r3, full):
    copies = [wire.go(pack.at[c, x], r1.at[n], me.at(core=c, x=x)) for n, (c, x) in enumerate(others(me))]
    yield
    for copy in copies:
        copy.wait_recv()
    total = pack[me.core, me.x] + r1[0]
    for n in range(1, 7):
        total = total + r1[n]
    pack[me.core, me.x] = total
    copies = [wire.go(pack.at[me.core, me.x, me.ys(d)], r2.at[d - 1], me.at(y=me.ys(d))) for d in (2, 1, 3)]
    yield
    for copy in copies:
        copy.wait_recv()
    r3[me.z] = pack[me.core, me.x, me.y] + r2[0] + r2[1] + r2[2]
    copies = [wire.go(r3.at[me.z], r3.at[me.z], me.at(z=me.zs(d))) for d in (4, 3, 5, 2, 6, 1, 7)]
    yield
    for copy in copies:
        copy.wait_recv()
    total = r3[0]
    for n in range(1, 8):
        total = total + r3[n]
    full[me.core, me.x, me.y] = total
    view = full.at[me.core, me.x, me.y]
    copies = [wire.go(view, view, me.at(y=me.ys(d))) for d in (2, 1, 3)]
    yield
    for copy in copies:
        copy.wait_recv()
    view = full.at[me.core, me.x]
    copies = [wire.go(view, view, me.at(core=c, x=x)) for c, x in others(me)]
    yield
    for copy in copies:
        copy.wait_recv()
    yield


def return_kernel(
    back_ref, feat_ref, gp_ref, ws_ref, wn_ref, gself_ref, gbias_ref,
    gf_ref, gs_ref, gn_ref,
    sums, rc, yl1, yr1, yl2, yr2, zin, zrel, pack_s, a1, a2, a3, pack_n, b1, b2, b3, send, recv,
):
    me = Place()
    wire = Wire(send, recv)
    up, down = me.at(y=me.ys(1)), me.at(y=me.ys(3))
    far, near = me.at(z=me.zs(2)), me.at(z=me.zs(6))
    partner = me.partner()
    peers = [me.at(core=c, x=x) for c, x in others(me)]
    peers += [me.at(y=me.ys(d)) for d in (1, 2, 3)]
    peers += [me.at(z=me.zs(d)) for d in range(1, 8)]
    barrier = greet(peers)
    other = 1 - me.zh
    order = [(other, 2), (me.zh, 2), (other, 1), (other, 3), (me.zh, 1), (me.zh, 3), (other, 0), (me.zh, 0)]

    def group(zh, d):
        return zh * 4 + me.ys(d)

    pack_rows(pack_s, gself_ref[...])
    pack_s[:, :, :, pl.ds(8, 8), :] = jnp.zeros((2, 4, 4, 8, TILE), F32)
    pack_s[0, 0, 0, pl.ds(8, 1), :] = gbias_ref[...]
    pl.semaphore_wait(barrier, len(peers))

    from_core = {}
    for n, (zh, d) in enumerate(order):
        g = group(zh, d)
        from_core[n] = wire.go(back_ref.at[g, 1 - me.core], rc.at[g], partner)

    early = total_over_all(me, wire, pack_s, a1, a2, a3, gs_ref)
    next(early)
    gf_ref[...] = dot_f32(gp_ref[...], ws_ref[...], ((1,), (1,)))

    def summed(n):
        zh, d = order[n]
        g = group(zh, d)
        from_core[n].wait_recv()
        sums[g] = back_ref[g, me.core] + rc[g]
        return g

    low, high = pl.ds(0, HALF), pl.ds(HALF, HALF)
    firsts = []
    for n in (0, 1):
        g = summed(n)
        firsts.append((wire.go(sums.at[g, low], yl1.at[n], up), wire.go(sums.at[g, high], yr1.at[n], down)))
    next(early)
    seconds = []
    for n in (0, 1):
        g = summed(2 + 2 * n)
        firsts[n][0].wait_recv()
        sums[g, low, :] += yl1[n]
        one = wire.go(sums.at[g], yl2.at[n], up)
        g = summed(3 + 2 * n)
        firsts[n][1].wait_recv()
        sums[g, high, :] += yr1[n]
        two = wire.go(sums.at[g], yr2.at[n], down)
        seconds.append((one, two))
        next(early)

    def finished(n):
        g = summed(6 + n)
        seconds[n][0].wait_recv()
        seconds[n][1].wait_recv()
        sums[g] += yl2[n] + yr2[n]
        return g

    g = finished(0)
    z_up = wire.go(sums.at[g, low], zrel.at[0], far)
    z_down = wire.go(sums.at[g, high], zrel.at[1], near)
    next(early)
    z_up.wait_recv()
    zf_up = wire.go(zrel.at[0], zin.at[low], far)
    z_down.wait_recv()
    zf_down = wire.go(zrel.at[1], zin.at[high], near)
    g = finished(1)
    zf_up.wait_recv()
    zf_down.wait_recv()
    back_rows = sums[g] + zin[...]

    pack_rows(pack_n, dot_f32(feat_ref[...], back_rows, ((0,), (0,))))
    late = total_over_all(me, wire, pack_n, b1, b2, b3, gn_ref)
    next(late)
    gf_ref[...] += dot_f32(back_rows, wn_ref[...], ((1,), (1,)))
    next(early)
    for _ in range(5):
        next(late)
    wire.drain()


def finish_kernel(factor, gf_ref, gs_ref, gn_ref, gf_out, gs_out, gn_out, gb_out, sem):
    copy = pltpu.make_async_copy(gf_ref, gf_out, sem.at[0])
    copy.start()
    for n in range(32):
        place = (n // 16, n // 4 % 4, n % 4)
        gs_out[pl.ds(n * 8, 8), :] = gs_ref[place][:8] * factor
        gn_out[pl.ds(n * 8, 8), :] = gn_ref[place] * factor
    gb_out[...] = gs_ref[0, 0, 0, pl.ds(8, 1), :] * factor
    copy.wait()


def local(features, self_weight, neigh_weight, out_bias, adjacency_tiles, tile_columns, live_counts, cotangent):
    vmem = pl.BlockSpec(memory_space=pltpu.VMEM)
    smem = pl.BlockSpec(memory_space=pltpu.SMEM)
    hbm = pl.BlockSpec(memory_space=pltpu.HBM)
    fin, fout = self_weight.shape

    def shape(*dims, dtype=F32):
        return jax.ShapeDtypeStruct(dims, dtype)

    dma = pltpu.SemaphoreType.DMA
    cols = tile_columns.T
    hidden, grad_pre, scaled, adjt, gself, gbias, feat, ws, wn = pl.pallas_call(
        forward_kernel,
        out_shape=[
            shape(BLK, fout),
            shape(BLK, fout),
            shape(GRID, BLK, fout),
            shape(TROWS, 2 * TILE, TILE, dtype=BF16),
            shape(fin, fout),
            shape(1, fout),
            shape(BLK, fin),
            shape(fin, fout),
            shape(fin, fout),
        ],
        in_specs=[hbm] * 8,
        out_specs=[vmem] * 9,
        scratch_shapes=[
            pltpu.VMEM((TROWS, TILE, fout), F32),
            pltpu.VMEM((TROWS, TILE, 2 * TILE), BF16),
            pltpu.VMEM((GRID, BLK + DEG, fout), F32),
            pltpu.VMEM((4, HALF, fout), F32),
            pltpu.VMEM((4, HALF + DEG, fout), F32),
            pltpu.VMEM((4, BLK + DEG, fout), F32),
            pltpu.VMEM((4, BLK + DEG, fout), F32),
            pltpu.VMEM((3, BLK + DEG, fout), F32),
            pltpu.VMEM((2, TPB // 2, TILE, fout), F32),
            pltpu.VMEM((BLK, fout), F32),
            pltpu.VMEM((2, TPB, 2, TILE, TILE), jnp.int32),
            pltpu.VMEM((1, fout), F32),
            pltpu.VMEM((BLK, fout), F32),
            pltpu.SMEM((2, TROWS), jnp.int32),
            pltpu.SMEM((1, TROWS), jnp.int32),
            dma((2,)),
            dma((7,)),
            dma((FWD_COPIES,)),
            dma((FWD_COPIES,)),
        ],
        compiler_params=pltpu.CompilerParams(collective_id=0, has_side_effects=True, vmem_limit_bytes=24 << 20),
        name="forward",
    )(
        *(
            pltpu.with_memory_space_constraint(given, pltpu.HBM)
            for given in (
                cols,
                live_counts.T,
                features,
                self_weight,
                neigh_weight,
                out_bias.reshape(1, fout),
                cotangent,
                adjacency_tiles,
            )
        ),
    )

    steps = 8
    rows = TROWS // steps
    back, hidden = pl.pallas_call(
        backward_kernel,
        grid=(steps,),
        out_shape=[shape(TROWS, TILE, fout), shape(BLK, fout)],
        in_specs=[
            smem,
            pl.BlockSpec((rows, 2 * TILE, TILE), lambda i: (i, 0, 0)),
            pl.BlockSpec((rows, TILE, fout), lambda i: (i, 0, 0)),
            pl.BlockSpec(memory_space=pl.ANY),
        ],
        out_specs=[pl.BlockSpec((TROWS, TILE, fout), lambda i: (0, 0, 0)), pl.BlockSpec(memory_space=pltpu.HBM)],
        scratch_shapes=[dma((1,))],
        compiler_params=pltpu.CompilerParams(vmem_limit_bytes=16 << 20),
        name="backward",
    )(cols, adjt, scaled.reshape(TROWS, TILE, fout), hidden)

    grad_features, total_self, total_neigh = pl.pallas_call(
        return_kernel,
        out_shape=[shape(BLK, fin), shape(2, 4, 4, 16, fout), shape(2, 4, 4, 8, fout)],
        in_specs=[vmem] * 7,
        out_specs=[vmem] * 3,
        scratch_shapes=[
            pltpu.VMEM((8, BLK, fout), F32),
            pltpu.VMEM((8, BLK, fout), F32),
            pltpu.VMEM((2, HALF, fout), F32),
            pltpu.VMEM((2, HALF, fout), F32),
            pltpu.VMEM((2, BLK, fout), F32),
            pltpu.VMEM((2, BLK, fout), F32),
            pltpu.VMEM((BLK, fout), F32),
            pltpu.VMEM((2, HALF, fout), F32),
            pltpu.VMEM((2, 4, 4, 16, fout), F32),
            pltpu.VMEM((7, 4, 16, fout), F32),
            pltpu.VMEM((3, 16, fout), F32),
            pltpu.VMEM((8, 16, fout), F32),
            pltpu.VMEM((2, 4, 4, 8, fout), F32),
            pltpu.VMEM((7, 4, 8, fout), F32),
            pltpu.VMEM((3, 8, fout), F32),
            pltpu.VMEM((8, 8, fout), F32),
            dma((BACK_COPIES,)),
            dma((BACK_COPIES,)),
        ],
        compiler_params=pltpu.CompilerParams(collective_id=1, has_side_effects=True, vmem_limit_bytes=24 << 20),
        name="backward_return",
    )(back.reshape(8, 2, BLK, fout), feat, grad_pre, ws, wn, gself, gbias)

    nodes = BLK * lax.axis_size("row") * lax.axis_size("col")
    factor = 1.0 / math.sqrt(nodes)
    grad_features, grad_self, grad_neigh, grad_bias = pl.pallas_call(
        lambda *refs: finish_kernel(factor, *refs),
        out_shape=[shape(BLK, fin), shape(fin, fout), shape(fin, fout), shape(1, fout)],
        in_specs=[pl.BlockSpec(memory_space=pl.ANY), vmem, vmem],
        out_specs=[pl.BlockSpec(memory_space=pltpu.HBM), vmem, vmem, vmem],
        scratch_shapes=[dma((1,))],
        compiler_params=pltpu.CompilerParams(vmem_limit_bytes=8 << 20),
        name="finish",
    )(grad_features, total_self, total_neigh)
    return hidden, grad_features, grad_self, grad_neigh, grad_bias.reshape(fout)


def solution(mesh):
    return jax.shard_map(
        local,
        mesh=mesh,
        in_specs=(
            P(("row", "col"), None),
            P(),
            P(),
            P(),
            P("row", "col", None, None),
            P("row", "col"),
            P("row", "col"),
            P(("row", "col"), None),
        ),
        out_specs=(P(("row", "col"), None), P(("row", "col"), None), P(), P(), P()),
        check_vma=False,
    )
```

```python
import math

import jax
import jax.numpy as jnp
from jax import lax
from jax.experimental import pallas as pl
from jax.experimental.pallas import tpu as pltpu
from jax.sharding import PartitionSpec as P

MESH = pl.DeviceIdType.MESH
F32 = jnp.float32
BF16 = jnp.bfloat16
HIGHEST = lax.Precision.HIGHEST

BLK = 512
HALF = BLK // 2
TILE = 128
TPB = BLK // TILE
GRID = 16
TROWS = TPB * GRID
DEG = 8


class Place:
    def __init__(self):
        row, col = lax.axis_index("row"), lax.axis_index("col")
        self.row, self.col = row, col
        self.core = lax.rem(row, 2)
        self.y = lax.rem(lax.div(row, 2), 4)
        self.zh = lax.div(row, 8)
        self.x = lax.rem(col, 4)
        self.zl = lax.div(col, 4)
        self.z = self.zh * 4 + self.zl

    def at(self, core=None, y=None, z=None, x=None):
        core = self.core if core is None else core
        y = self.y if y is None else y
        z = self.z if z is None else z
        x = self.x if x is None else x
        return (lax.div(z, 4) * 4 + y) * 2 + core, lax.rem(z, 4) * 4 + x

    def partner(self):
        return self.at(core=1 - self.core)

    def ys(self, step):
        return lax.rem(self.y + step, 4)

    def xs(self, step):
        return lax.rem(self.x + step, 4)

    def zs(self, step):
        return lax.rem(self.z + step, 8)

    def zline(self, step):
        return lax.rem(self.zl + step, 4)


class Wire:
    def __init__(self, send, recv):
        self.send, self.recv, self.copies = send, recv, []

    def go(self, src, dst, device):
        i = len(self.copies)
        copy = pltpu.make_async_remote_copy(
            src_ref=src,
            dst_ref=dst,
            send_sem=self.send.at[i],
            recv_sem=self.recv.at[i],
            device_id=device,
            device_id_type=MESH,
        )
        copy.start()
        self.copies.append(copy)
        return copy

    def drain(self):
        for copy in self.copies:
            copy.wait_send()


def greet(peers):
    barrier = pltpu.get_barrier_semaphore()
    for peer in peers:
        pl.semaphore_signal(barrier, inc=1, device_id=peer, device_id_type=MESH)
    return barrier


def split(value):
    high = value.astype(BF16)
    low = (value - high.astype(F32)).astype(BF16)
    return jnp.concatenate([high, low], axis=1)


def dot_f32(a, b, dims):
    return lax.dot_general(a, b, (dims, ((), ())), precision=HIGHEST, preferred_element_type=F32)


FWD_COPIES = 21 + 19 + 19


def forward_kernel(
    cols_hbm, live_hbm, feat_hbm, ws_hbm, wn_hbm, bias_hbm, cot_hbm, adj_ref,
    hid_ref, gp_ref, sall_ref, adjt_ref, gself_ref, gbias_ref, feat_out, ws_out, wn_out,
    hall, adjb, part, xl1, xr1, xl2, xr2, zin, zrel, selfp, stage, bias_ref, cot_ref, cols_ref, live_ref, stage_sem, load_sem, send, recv,
):
    feat_ref, ws_ref, wn_ref = feat_out, ws_out, wn_out
    pairs = ((feat_hbm, feat_ref), (wn_hbm, wn_ref), (ws_hbm, ws_ref), (bias_hbm, bias_ref), (cot_hbm, cot_ref))
    pairs += ((live_hbm, live_ref), (cols_hbm, cols_ref))
    loads = [pltpu.make_async_copy(a, b, load_sem.at[i]) for i, (a, b) in enumerate(pairs)]
    for load in loads:
        load.start()
    me = Place()
    wire = Wire(send, recv)
    right, left = me.at(x=me.xs(1)), me.at(x=me.xs(3))
    up, down = me.at(y=me.ys(1)), me.at(y=me.ys(3))
    far, near = me.at(z=me.zs(2)), me.at(z=me.zs(6))
    line = {d: me.at(z=me.zh * 4 + me.zline(d)) for d in (1, 2, 3)}
    peers = [me.partner(), up, down, right, left, far, near, line[1], line[2], line[3]]
    barrier = greet(peers)

    def fetch(chunk, slot):
        return pltpu.make_async_copy(adj_ref.at[pl.ds(chunk * TPB, TPB)], stage.at[slot], stage_sem.at[slot])

    fetch(0, 0).start()
    fetch(1, 1).start()

    def block(row):
        return hall.at[pl.ds(row * TPB, TPB)]

    def block_half(row, half):
        return hall.at[pl.ds(row * TPB + half * (TPB // 2), TPB // 2)]

    def row_of(y, zh, core):
        return (zh * 4 + y) * 2 + core

    loads[0].wait()
    loads[1].wait()
    own = dot_f32(feat_ref[...], wn_ref[...], ((1,), (0,)))
    hall[pl.ds(me.row * TPB, TPB)] = own.reshape(TPB, TILE, TILE)
    pl.semaphore_wait(barrier, len(peers))

    partner = me.partner()

    def mine(y, zh):
        return row_of(y, zh, me.core)

    def share(y, zh):
        return wire.go(block(mine(y, zh)), block(mine(y, zh)), partner)

    z_up = wire.go(block_half(me.row, 0), zrel.at[0], far)
    z_down = wire.go(block_half(me.row, 1), zrel.at[1], near)
    y_up = wire.go(block(me.row), block(me.row), up)
    y_down = wire.go(block(me.row), block(me.row), down)
    shared = [share(me.y, me.zh)]

    def convert(chunk, carry):
        slot = lax.rem(chunk, 2)
        fetch(chunk, slot).wait()
        degrees = []
        for i in range(TPB):
            t = chunk * TPB + i
            live = live_ref[0, t]
            tiles = [jnp.where(live > k, stage[slot, i, k].astype(F32), 0.0) for k in range(2)]
            turned = [tile.T for tile in tiles]
            degrees.append(jnp.sum(turned[0] + turned[1], axis=0, keepdims=True))
            adjb[t] = jnp.concatenate(tiles, axis=1).astype(BF16)
            adjt_ref[t] = jnp.concatenate(turned, axis=0).astype(BF16)
        part[chunk, BLK:, :] = jnp.concatenate(degrees + [jnp.zeros((DEG - TPB, TILE), F32)], axis=0)

        @pl.when(chunk + 2 < GRID)
        def _():
            fetch(chunk + 2, slot).start()

        return carry

    for load in loads[2:]:
        load.wait()
    lax.fori_loop(0, 4, convert, 0)
    z_up.wait_recv()
    source = mine(me.y, lax.div(me.zs(6), 4))
    zf_up = wire.go(zrel.at[0], block_half(source, 0), far)
    z_down.wait_recv()
    source = mine(me.y, lax.div(me.zs(2), 4))
    zf_down = wire.go(zrel.at[1], block_half(source, 1), near)
    lax.fori_loop(4, 7, convert, 0)

    def relay(zh, first, second):
        first.wait_recv()
        row = mine(me.ys(3), zh)
        one = wire.go(block_half(row, 0), block_half(row, 0), up)
        shared.append(share(me.ys(3), zh))
        second.wait_recv()
        row = mine(me.ys(1), zh)
        two = wire.go(block_half(row, 1), block_half(row, 1), down)
        shared.append(share(me.ys(1), zh))
        return one, two

    relays = relay(me.zh, y_up, y_down)
    lax.fori_loop(7, 11, convert, 0)
    other = 1 - me.zh
    zf_up.wait_recv()
    zf_down.wait_recv()
    row = mine(me.y, other)
    y_up = wire.go(block(row), block(row), up)
    y_down = wire.go(block(row), block(row), down)
    shared.append(share(me.y, other))
    relays[0].wait_recv()
    relays[1].wait_recv()
    shared.append(share(me.ys(2), me.zh))
    lax.fori_loop(11, GRID, convert, 0)
    relays = relay(other, y_up, y_down)
    selfp[...] = dot_f32(feat_ref[...], ws_ref[...], ((1,), (0,)))
    relays[0].wait_recv()
    relays[1].wait_recv()
    shared.append(share(me.ys(2), other))
    for copy in shared:
        copy.wait_recv()

    def multiply(zl, x):
        shard = zl * 4 + x

        def tile_row(i, carry):
            t = shard * TPB + i
            picked = jnp.concatenate([hall[cols_ref[0, t]], hall[cols_ref[1, t]]], axis=0)
            both = jnp.dot(adjb[t], split(picked), preferred_element_type=F32)
            part[shard, pl.ds(pl.multiple_of(i * TILE, TILE), TILE), :] = both[:, :TILE] + both[:, TILE:]
            return carry

        lax.fori_loop(0, TPB, tile_row, 0)
        return shard

    order = (2, 1, 3, 0)
    low, high = pl.ds(0, HALF), pl.ds(HALF, HALF + DEG)
    firsts = []
    for d in order:
        shard = multiply(me.zline(d), me.xs(2))
        firsts.append(
            (
                wire.go(part.at[shard, low], xl1.at[d], right),
                wire.go(part.at[shard, high], xr1.at[d], left),
            )
        )
    seconds = []
    for d, (from_left, from_right) in zip(order, firsts):
        shard = multiply(me.zline(d), me.xs(1))
        from_left.wait_recv()
        part[shard, low, :] += xl1[d]
        one = wire.go(part.at[shard], xl2.at[d], right)
        shard = multiply(me.zline(d), me.xs(3))
        from_right.wait_recv()
        part[shard, high, :] += xr1[d]
        two = wire.go(part.at[shard], xr2.at[d], left)
        seconds.append((one, two))
    for d in order:
        multiply(me.zline(d), me.x)
    arrivals = []
    for d, (from_left, from_right) in zip(order, seconds):
        shard = me.zline(d) * 4 + me.x
        from_left.wait_recv()
        from_right.wait_recv()
        part[shard] += xl2[d] + xr2[d]
        if d:
            arrivals.append(wire.go(part.at[shard], zin.at[d - 1], line[d]))
    for copy in arrivals:
        copy.wait_recv()
    total = part[me.col] + zin[0] + zin[1] + zin[2]

    for i in range(TPB):
        rows = pl.ds(i * TILE, TILE)
        counts = jnp.broadcast_to(total[BLK + i : BLK + i + 1, :], (TILE, TILE)).T
        degree = 1.0 + counts
        pre = selfp[rows, :] + total[i * TILE : (i + 1) * TILE, :] / degree + bias_ref[...]
        sig = jax.nn.sigmoid(pre)
        hid_ref[rows, :] = pre * sig
        grad = cot_ref[rows, :] * sig * (1.0 + pre * (1.0 - sig))
        gp_ref[rows, :] = grad
        sall_ref[me.col, rows, :] = grad / degree

    def spread(block_col):
        return (
            wire.go(sall_ref.at[block_col], sall_ref.at[block_col], right),
            wire.go(sall_ref.at[block_col], sall_ref.at[block_col], left),
        )

    def pass_on(zl, pair):
        pair[0].wait_recv()
        from_left = zl * 4 + me.xs(3)
        one = wire.go(sall_ref.at[from_left, pl.ds(0, HALF)], sall_ref.at[from_left, pl.ds(0, HALF)], right)
        pair[1].wait_recv()
        from_right = zl * 4 + me.xs(1)
        two = wire.go(sall_ref.at[from_right, pl.ds(HALF, HALF)], sall_ref.at[from_right, pl.ds(HALF, HALF)], left)
        return one, two

    sent = {d: wire.go(sall_ref.at[me.col], sall_ref.at[me.col], line[d]) for d in (1, 3, 2)}
    pending = [(me.zl, spread(me.col))]
    gself_ref[...] = dot_f32(feat_ref[...], gp_ref[...], ((0,), (0,)))
    gbias_ref[...] = jnp.sum(gp_ref[...], axis=0, keepdims=True)
    last = []
    for d in (1, 3, 2):
        zl = me.zline(4 - d)
        sent[d].wait_recv()
        pending.append((zl, spread(zl * 4 + me.x)))
        last += pass_on(*pending.pop(0))
    last += pass_on(*pending.pop(0))
    for copy in last:
        copy.wait_recv()
    wire.drain()


def backward_kernel(cols_ref, adjt_ref, scaled_ref, hid_ref, back_ref, hid_out, hid_sem):
    step = pl.program_id(0)
    rows = scaled_ref.shape[0]
    hidden = pltpu.make_async_copy(hid_ref, hid_out, hid_sem.at[0])

    @pl.when(step == 0)
    def _():
        hidden.start()
        back_ref[...] = jnp.zeros_like(back_ref)

    for start in range(0, rows, 4):
        parts = []
        for i in range(start, start + 4):
            both = jnp.dot(adjt_ref[i], split(scaled_ref[i]), preferred_element_type=F32)
            parts.append(both[:, :TILE] + both[:, TILE:])
        for i in range(start, start + 4):
            t = step * rows + i
            back_ref[cols_ref[0, t]] += parts[i - start][:TILE]
            back_ref[cols_ref[1, t]] += parts[i - start][TILE:]

    @pl.when(step == pl.num_programs(0) - 1)
    def _():
        hidden.wait()


SUM_COPIES = 7 + 3 + 7 + 3 + 7
LATE_COPIES = 31 + 7 + 31
BACK_COPIES = 8 + 8 + 4 + SUM_COPIES + LATE_COPIES


def others(me):
    return [(me.core, me.xs(2)), (1 - me.core, me.xs(2))] + [
        (me.core, me.xs(1)), (1 - me.core, me.xs(1)), (me.core, me.xs(3)), (1 - me.core, me.xs(3)), (1 - me.core, me.x)
    ]


def plane(me):
    return [
        (1 - me.core if dc else me.core, me.xs(dx), me.ys(dy))
        for dx in (2, 1, 3, 0)
        for dy in (2, 1, 3, 0)
        for dc in (1, 0)
        if dc or dx or dy
    ]


def pack_rows(pack, rows):
    for n in range(32):
        pack[n // 16, n // 4 % 4, n % 4, pl.ds(0, 8), :] = rows[n * 8 : (n + 1) * 8, :]


def total_over_all(me, wire, pack, r1, r2, r3, full):
    copies = [wire.go(pack.at[c, x], r1.at[n], me.at(core=c, x=x)) for n, (c, x) in enumerate(others(me))]
    yield
    for copy in copies:
        copy.wait_recv()
    total = pack[me.core, me.x] + r1[0]
    for n in range(1, 7):
        total = total + r1[n]
    pack[me.core, me.x] = total
    copies = [wire.go(pack.at[me.core, me.x, me.ys(d)], r2.at[d - 1], me.at(y=me.ys(d))) for d in (2, 1, 3)]
    yield
    for copy in copies:
        copy.wait_recv()
    r3[me.z] = pack[me.core, me.x, me.y] + r2[0] + r2[1] + r2[2]
    copies = [wire.go(r3.at[me.z], r3.at[me.z], me.at(z=me.zs(d))) for d in (4, 3, 5, 2, 6, 1, 7)]
    yield
    for copy in copies:
        copy.wait_recv()
    total = r3[0]
    for n in range(1, 8):
        total = total + r3[n]
    full[me.core, me.x, me.y] = total
    view = full.at[me.core, me.x, me.y]
    copies = [wire.go(view, view, me.at(y=me.ys(d))) for d in (2, 1, 3)]
    yield
    for copy in copies:
        copy.wait_recv()
    view = full.at[me.core, me.x]
    copies = [wire.go(view, view, me.at(core=c, x=x)) for c, x in others(me)]
    yield
    for copy in copies:
        copy.wait_recv()
    yield


def total_by_planes(me, wire, pack, r1, r3, full):
    copies = [wire.go(pack.at[c, x, y], r1.at[n], me.at(core=c, x=x, y=y)) for n, (c, x, y) in enumerate(plane(me))]
    yield
    for copy in copies:
        copy.wait_recv()
    total = pack[me.core, me.x, me.y]
    for n in range(31):
        total = total + r1[n]
    r3[me.z] = total
    copies = [wire.go(r3.at[me.z], r3.at[me.z], me.at(z=me.zs(d))) for d in (4, 3, 5, 2, 6, 1, 7)]
    yield
    for copy in copies:
        copy.wait_recv()
    total = r3[0]
    for n in range(1, 8):
        total = total + r3[n]
    full[me.core, me.x, me.y] = total
    view = full.at[me.core, me.x, me.y]
    copies = [wire.go(view, view, me.at(core=c, x=x, y=y)) for c, x, y in plane(me)]
    yield
    for copy in copies:
        copy.wait_recv()
    yield


def return_kernel(
    back_ref, feat_ref, gp_ref, ws_ref, wn_ref, gself_ref, gbias_ref,
    gf_ref, gs_ref, gn_ref,
    sums, rc, yl1, yr1, yl2, yr2, zin, zrel, pack_s, a1, a2, a3, pack_n, b1, b3, send, recv,
):
    me = Place()
    wire = Wire(send, recv)
    up, down = me.at(y=me.ys(1)), me.at(y=me.ys(3))
    far, near = me.at(z=me.zs(2)), me.at(z=me.zs(6))
    partner = me.partner()
    peers = [me.at(core=c, x=x, y=y) for c, x, y in plane(me)]
    peers += [me.at(z=me.zs(d)) for d in range(1, 8)]
    barrier = greet(peers)
    other = 1 - me.zh
    order = [(other, 2), (me.zh, 2), (other, 1), (other, 3), (me.zh, 1), (me.zh, 3), (other, 0), (me.zh, 0)]

    def group(zh, d):
        return zh * 4 + me.ys(d)

    pack_rows(pack_s, gself_ref[...])
    pack_s[:, :, :, pl.ds(8, 8), :] = jnp.zeros((2, 4, 4, 8, TILE), F32)
    pack_s[0, 0, 0, pl.ds(8, 1), :] = gbias_ref[...]
    pl.semaphore_wait(barrier, len(peers))

    early = total_over_all(me, wire, pack_s, a1, a2, a3, gs_ref)
    next(early)
    from_core = {}
    for n, (zh, d) in enumerate(order):
        g = group(zh, d)
        from_core[n] = wire.go(back_ref.at[g, 1 - me.core], rc.at[g], partner)

    gf_ref[...] = dot_f32(gp_ref[...], ws_ref[...], ((1,), (1,)))

    def summed(n):
        zh, d = order[n]
        g = group(zh, d)
        from_core[n].wait_recv()
        sums[g] = back_ref[g, me.core] + rc[g]
        return g

    low, high = pl.ds(0, HALF), pl.ds(HALF, HALF)
    firsts = []
    for n in (0, 1):
        g = summed(n)
        firsts.append((wire.go(sums.at[g, low], yl1.at[n], up), wire.go(sums.at[g, high], yr1.at[n], down)))
    seconds = []
    for n in (0, 1):
        g = summed(2 + 2 * n)
        firsts[n][0].wait_recv()
        sums[g, low, :] += yl1[n]
        one = wire.go(sums.at[g], yl2.at[n], up)
        g = summed(3 + 2 * n)
        firsts[n][1].wait_recv()
        sums[g, high, :] += yr1[n]
        two = wire.go(sums.at[g], yr2.at[n], down)
        seconds.append((one, two))
        next(early)

    def finished(n):
        g = summed(6 + n)
        seconds[n][0].wait_recv()
        seconds[n][1].wait_recv()
        sums[g] += yl2[n] + yr2[n]
        return g

    g = finished(0)
    z_up = wire.go(sums.at[g, low], zrel.at[0], far)
    z_down = wire.go(sums.at[g, high], zrel.at[1], near)
    next(early)
    z_up.wait_recv()
    zf_up = wire.go(zrel.at[0], zin.at[low], far)
    z_down.wait_recv()
    zf_down = wire.go(zrel.at[1], zin.at[high], near)
    next(early)
    g = finished(1)
    zf_up.wait_recv()
    zf_down.wait_recv()
    back_rows = sums[g] + zin[...]

    pack_rows(pack_n, dot_f32(feat_ref[...], back_rows, ((0,), (0,))))
    late = total_by_planes(me, wire, pack_n, b1, b3, gn_ref)
    next(late)
    gf_ref[...] += dot_f32(back_rows, wn_ref[...], ((1,), (1,)))
    next(early)
    for _ in range(3):
        next(late)
    wire.drain()


def finish_kernel(factor, gf_ref, gs_ref, gn_ref, gf_out, gs_out, gn_out, gb_out, sem):
    copy = pltpu.make_async_copy(gf_ref, gf_out, sem.at[0])
    copy.start()
    for n in range(32):
        place = (n // 16, n // 4 % 4, n % 4)
        gs_out[pl.ds(n * 8, 8), :] = gs_ref[place][:8] * factor
        gn_out[pl.ds(n * 8, 8), :] = gn_ref[place] * factor
    gb_out[...] = gs_ref[0, 0, 0, pl.ds(8, 1), :] * factor
    copy.wait()


def local(features, self_weight, neigh_weight, out_bias, adjacency_tiles, tile_columns, live_counts, cotangent):
    vmem = pl.BlockSpec(memory_space=pltpu.VMEM)
    smem = pl.BlockSpec(memory_space=pltpu.SMEM)
    hbm = pl.BlockSpec(memory_space=pltpu.HBM)
    fin, fout = self_weight.shape

    def shape(*dims, dtype=F32):
        return jax.ShapeDtypeStruct(dims, dtype)

    dma = pltpu.SemaphoreType.DMA
    cols = tile_columns.T
    hidden, grad_pre, scaled, adjt, gself, gbias, feat, ws, wn = pl.pallas_call(
        forward_kernel,
        out_shape=[
            shape(BLK, fout),
            shape(BLK, fout),
            shape(GRID, BLK, fout),
            shape(TROWS, 2 * TILE, TILE, dtype=BF16),
            shape(fin, fout),
            shape(1, fout),
            shape(BLK, fin),
            shape(fin, fout),
            shape(fin, fout),
        ],
        in_specs=[hbm] * 8,
        out_specs=[vmem] * 9,
        scratch_shapes=[
            pltpu.VMEM((TROWS, TILE, fout), F32),
            pltpu.VMEM((TROWS, TILE, 2 * TILE), BF16),
            pltpu.VMEM((GRID, BLK + DEG, fout), F32),
            pltpu.VMEM((4, HALF, fout), F32),
            pltpu.VMEM((4, HALF + DEG, fout), F32),
            pltpu.VMEM((4, BLK + DEG, fout), F32),
            pltpu.VMEM((4, BLK + DEG, fout), F32),
            pltpu.VMEM((3, BLK + DEG, fout), F32),
            pltpu.VMEM((2, TPB // 2, TILE, fout), F32),
            pltpu.VMEM((BLK, fout), F32),
            pltpu.VMEM((2, TPB, 2, TILE, TILE), jnp.int32),
            pltpu.VMEM((1, fout), F32),
            pltpu.VMEM((BLK, fout), F32),
            pltpu.SMEM((2, TROWS), jnp.int32),
            pltpu.SMEM((1, TROWS), jnp.int32),
            dma((2,)),
            dma((7,)),
            dma((FWD_COPIES,)),
            dma((FWD_COPIES,)),
        ],
        compiler_params=pltpu.CompilerParams(collective_id=0, has_side_effects=True, vmem_limit_bytes=24 << 20),
        name="forward",
    )(
        *(
            pltpu.with_memory_space_constraint(given, pltpu.HBM)
            for given in (
                cols,
                live_counts.T,
                features,
                self_weight,
                neigh_weight,
                out_bias.reshape(1, fout),
                cotangent,
                adjacency_tiles,
            )
        ),
    )

    steps = 8
    rows = TROWS // steps
    back, hidden = pl.pallas_call(
        backward_kernel,
        grid=(steps,),
        out_shape=[shape(TROWS, TILE, fout), shape(BLK, fout)],
        in_specs=[
            smem,
            pl.BlockSpec((rows, 2 * TILE, TILE), lambda i: (i, 0, 0)),
            pl.BlockSpec((rows, TILE, fout), lambda i: (i, 0, 0)),
            pl.BlockSpec(memory_space=pl.ANY),
        ],
        out_specs=[pl.BlockSpec((TROWS, TILE, fout), lambda i: (0, 0, 0)), pl.BlockSpec(memory_space=pltpu.HBM)],
        scratch_shapes=[dma((1,))],
        compiler_params=pltpu.CompilerParams(vmem_limit_bytes=16 << 20),
        name="backward",
    )(cols, adjt, scaled.reshape(TROWS, TILE, fout), hidden)

    grad_features, total_self, total_neigh = pl.pallas_call(
        return_kernel,
        out_shape=[shape(BLK, fin), shape(2, 4, 4, 16, fout), shape(2, 4, 4, 8, fout)],
        in_specs=[vmem] * 7,
        out_specs=[vmem] * 3,
        scratch_shapes=[
            pltpu.VMEM((8, BLK, fout), F32),
            pltpu.VMEM((8, BLK, fout), F32),
            pltpu.VMEM((2, HALF, fout), F32),
            pltpu.VMEM((2, HALF, fout), F32),
            pltpu.VMEM((2, BLK, fout), F32),
            pltpu.VMEM((2, BLK, fout), F32),
            pltpu.VMEM((BLK, fout), F32),
            pltpu.VMEM((2, HALF, fout), F32),
            pltpu.VMEM((2, 4, 4, 16, fout), F32),
            pltpu.VMEM((7, 4, 16, fout), F32),
            pltpu.VMEM((3, 16, fout), F32),
            pltpu.VMEM((8, 16, fout), F32),
            pltpu.VMEM((2, 4, 4, 8, fout), F32),
            pltpu.VMEM((31, 8, fout), F32),
            pltpu.VMEM((8, 8, fout), F32),
            dma((BACK_COPIES,)),
            dma((BACK_COPIES,)),
        ],
        compiler_params=pltpu.CompilerParams(collective_id=1, has_side_effects=True, vmem_limit_bytes=24 << 20),
        name="backward_return",
    )(back.reshape(8, 2, BLK, fout), feat, grad_pre, ws, wn, gself, gbias)

    nodes = BLK * lax.axis_size("row") * lax.axis_size("col")
    factor = 1.0 / math.sqrt(nodes)
    grad_features, grad_self, grad_neigh, grad_bias = pl.pallas_call(
        lambda *refs: finish_kernel(factor, *refs),
        out_shape=[shape(BLK, fin), shape(fin, fout), shape(fin, fout), shape(1, fout)],
        in_specs=[pl.BlockSpec(memory_space=pl.ANY), vmem, vmem],
        out_specs=[pl.BlockSpec(memory_space=pltpu.HBM), vmem, vmem, vmem],
        scratch_shapes=[dma((1,))],
        compiler_params=pltpu.CompilerParams(vmem_limit_bytes=8 << 20),
        name="finish",
    )(grad_features, total_self, total_neigh)
    return hidden, grad_features, grad_self, grad_neigh, grad_bias.reshape(fout)


def solution(mesh):
    return jax.shard_map(
        local,
        mesh=mesh,
        in_specs=(
            P(("row", "col"), None),
            P(),
            P(),
            P(),
            P("row", "col", None, None),
            P("row", "col"),
            P("row", "col"),
            P(("row", "col"), None),
        ),
        out_specs=(P(("row", "col"), None), P(("row", "col"), None), P(), P(), P()),
        check_vma=False,
    )
```

```python
import math

import jax
import jax.numpy as jnp
from jax import lax
from jax.experimental import pallas as pl
from jax.experimental.pallas import tpu as pltpu
from jax.sharding import PartitionSpec as P

MESH = pl.DeviceIdType.MESH
F32 = jnp.float32
BF16 = jnp.bfloat16
HIGHEST = lax.Precision.HIGHEST

BLK = 512
HALF = BLK // 2
TILE = 128
TPB = BLK // TILE
GRID = 16
TROWS = TPB * GRID
DEG = 8


class Place:
    def __init__(self):
        row, col = lax.axis_index("row"), lax.axis_index("col")
        self.row, self.col = row, col
        self.core = lax.rem(row, 2)
        self.y = lax.rem(lax.div(row, 2), 4)
        self.zh = lax.div(row, 8)
        self.x = lax.rem(col, 4)
        self.zl = lax.div(col, 4)
        self.z = self.zh * 4 + self.zl

    def at(self, core=None, y=None, z=None, x=None):
        core = self.core if core is None else core
        y = self.y if y is None else y
        z = self.z if z is None else z
        x = self.x if x is None else x
        return (lax.div(z, 4) * 4 + y) * 2 + core, lax.rem(z, 4) * 4 + x

    def partner(self):
        return self.at(core=1 - self.core)

    def ys(self, step):
        return lax.rem(self.y + step, 4)

    def xs(self, step):
        return lax.rem(self.x + step, 4)

    def zs(self, step):
        return lax.rem(self.z + step, 8)

    def zline(self, step):
        return lax.rem(self.zl + step, 4)


class Wire:
    def __init__(self, send, recv):
        self.send, self.recv, self.copies = send, recv, []

    def go(self, src, dst, device):
        i = len(self.copies)
        copy = pltpu.make_async_remote_copy(
            src_ref=src,
            dst_ref=dst,
            send_sem=self.send.at[i],
            recv_sem=self.recv.at[i],
            device_id=device,
            device_id_type=MESH,
        )
        copy.start()
        self.copies.append(copy)
        return copy

    def drain(self):
        for copy in self.copies:
            copy.wait_send()


def greet(peers):
    barrier = pltpu.get_barrier_semaphore()
    for peer in peers:
        pl.semaphore_signal(barrier, inc=1, device_id=peer, device_id_type=MESH)
    return barrier


def split(value):
    high = value.astype(BF16)
    low = (value - high.astype(F32)).astype(BF16)
    return jnp.concatenate([high, low], axis=1)


def dot_f32(a, b, dims):
    return lax.dot_general(a, b, (dims, ((), ())), precision=HIGHEST, preferred_element_type=F32)


FWD_COPIES = 33 + 19 + 19


def forward_kernel(
    cols_hbm, live_hbm, feat_hbm, ws_hbm, wn_hbm, bias_hbm, cot_hbm, adj_ref,
    hid_ref, gp_ref, sall_ref, adjt_ref, gself_ref, gbias_ref, feat_out, ws_out, wn_out,
    hall, adjb, part, xl1, xr1, xl2, xr2, zin, zrel, selfp, stage, bias_ref, cot_ref, cols_ref, live_ref, stage_sem, load_sem, send, recv,
):
    feat_ref, ws_ref, wn_ref = feat_out, ws_out, wn_out
    pairs = ((feat_hbm, feat_ref), (wn_hbm, wn_ref), (ws_hbm, ws_ref), (bias_hbm, bias_ref), (cot_hbm, cot_ref))
    pairs += ((live_hbm, live_ref), (cols_hbm, cols_ref))
    loads = [pltpu.make_async_copy(a, b, load_sem.at[i]) for i, (a, b) in enumerate(pairs)]
    for load in loads:
        load.start()
    me = Place()
    wire = Wire(send, recv)
    right, left = me.at(x=me.xs(1)), me.at(x=me.xs(3))
    up, down = me.at(y=me.ys(1)), me.at(y=me.ys(3))
    far, near = me.at(z=me.zs(2)), me.at(z=me.zs(6))
    line = {d: me.at(z=me.zh * 4 + me.zline(d)) for d in (1, 2, 3)}
    peers = [me.partner(), up, down, right, left, far, near, line[1], line[2], line[3]]
    barrier = greet(peers)

    def fetch(chunk, slot):
        return pltpu.make_async_copy(adj_ref.at[pl.ds(chunk * TPB, TPB)], stage.at[slot], stage_sem.at[slot])

    fetch(0, 0).start()
    fetch(1, 1).start()

    def block(row):
        return hall.at[pl.ds(row * TPB, TPB)]

    def tile(row, i):
        return hall.at[row * TPB + i]

    def block_half(row, half):
        return hall.at[pl.ds(row * TPB + half * (TPB // 2), TPB // 2)]

    def row_of(y, zh, core):
        return (zh * 4 + y) * 2 + core

    loads[0].wait()
    loads[1].wait()
    own = dot_f32(feat_ref[...], wn_ref[...], ((1,), (0,)))
    hall[pl.ds(me.row * TPB, TPB)] = own.reshape(TPB, TILE, TILE)
    pl.semaphore_wait(barrier, len(peers))

    partner = me.partner()

    def mine(y, zh):
        return row_of(y, zh, me.core)

    def share(y, zh):
        return wire.go(block(mine(y, zh)), block(mine(y, zh)), partner)

    z_up = [wire.go(tile(me.row, p), zrel.at[0, p], far) for p in range(2)]
    z_down = [wire.go(tile(me.row, 2 + p), zrel.at[1, p], near) for p in range(2)]
    y_up = wire.go(block(me.row), block(me.row), up)
    y_down = wire.go(block(me.row), block(me.row), down)
    shared = [share(me.y, me.zh)]

    def convert(chunk, carry):
        slot = lax.rem(chunk, 2)
        fetch(chunk, slot).wait()
        degrees = []
        for i in range(TPB):
            t = chunk * TPB + i
            live = live_ref[0, t]
            tiles = [jnp.where(live > k, stage[slot, i, k].astype(F32), 0.0) for k in range(2)]
            turned = [tile.T for tile in tiles]
            degrees.append(jnp.sum(turned[0] + turned[1], axis=0, keepdims=True))
            adjb[t] = jnp.concatenate(tiles, axis=1).astype(BF16)
            adjt_ref[t] = jnp.concatenate(turned, axis=0).astype(BF16)
        part[chunk, BLK:, :] = jnp.concatenate(degrees + [jnp.zeros((DEG - TPB, TILE), F32)], axis=0)

        @pl.when(chunk + 2 < GRID)
        def _():
            fetch(chunk + 2, slot).start()

        return carry

    for load in loads[2:]:
        load.wait()
    zf_up, zf_down = [], []

    def onward(p):
        z_up[p].wait_recv()
        source = mine(me.y, lax.div(me.zs(6), 4))
        zf_up.append(wire.go(zrel.at[0, p], tile(source, p), far))
        z_down[p].wait_recv()
        source = mine(me.y, lax.div(me.zs(2), 4))
        zf_down.append(wire.go(zrel.at[1, p], tile(source, 2 + p), near))

    lax.fori_loop(0, 3, convert, 0)
    onward(0)
    lax.fori_loop(3, 5, convert, 0)
    onward(1)
    lax.fori_loop(5, 7, convert, 0)
    y_up.wait_recv()
    row = mine(me.ys(3), me.zh)
    near_up = wire.go(block_half(row, 0), block_half(row, 0), up)
    shared.append(share(me.ys(3), me.zh))
    y_down.wait_recv()
    row = mine(me.ys(1), me.zh)
    near_down = wire.go(block_half(row, 1), block_half(row, 1), down)
    shared.append(share(me.ys(1), me.zh))
    lax.fori_loop(7, 9, convert, 0)

    other = 1 - me.zh
    row = mine(me.y, other)
    y_up, y_down = [], []
    for p in range(2):
        zf_up[p].wait_recv()
        y_up.append(wire.go(tile(row, p), tile(row, p), up))
        zf_down[p].wait_recv()
        y_down.append(wire.go(tile(row, 2 + p), tile(row, 2 + p), down))
        lax.fori_loop(9 + p, 10 + p, convert, 0)
    y_up.append(wire.go(block_half(row, 1), block_half(row, 1), up))
    y_down.append(wire.go(block_half(row, 0), block_half(row, 0), down))
    shared.append(share(me.y, other))
    near_up.wait_recv()
    near_down.wait_recv()
    shared.append(share(me.ys(2), me.zh))
    lax.fori_loop(11, 13, convert, 0)
    below, above = mine(me.ys(3), other), mine(me.ys(1), other)
    far_up, far_down = [], []
    for p in range(2):
        y_up[p].wait_recv()
        far_up.append(wire.go(tile(below, p), tile(below, p), up))
        y_down[p].wait_recv()
        far_down.append(wire.go(tile(above, 2 + p), tile(above, 2 + p), down))
        lax.fori_loop(13 + p, 14 + p, convert, 0)
    lax.fori_loop(15, GRID, convert, 0)
    selfp[...] = dot_f32(feat_ref[...], ws_ref[...], ((1,), (0,)))
    y_up[2].wait_recv()
    shared.append(share(me.ys(3), other))
    y_down[2].wait_recv()
    shared.append(share(me.ys(1), other))
    row = mine(me.ys(2), other)
    for half, relayed in enumerate((far_up, far_down)):
        for copy in relayed:
            copy.wait_recv()
        shared.append(wire.go(block_half(row, half), block_half(row, half), partner))
    for copy in shared:
        copy.wait_recv()

    def multiply(zl, x):
        shard = zl * 4 + x

        def tile_row(i, carry):
            t = shard * TPB + i
            picked = jnp.concatenate([hall[cols_ref[0, t]], hall[cols_ref[1, t]]], axis=0)
            both = jnp.dot(adjb[t], split(picked), preferred_element_type=F32)
            part[shard, pl.ds(pl.multiple_of(i * TILE, TILE), TILE), :] = both[:, :TILE] + both[:, TILE:]
            return carry

        lax.fori_loop(0, TPB, tile_row, 0)
        return shard

    order = (2, 1, 3, 0)
    low, high = pl.ds(0, HALF), pl.ds(HALF, HALF + DEG)
    firsts = []
    for d in order:
        shard = multiply(me.zline(d), me.xs(2))
        firsts.append(
            (
                wire.go(part.at[shard, low], xl1.at[d], right),
                wire.go(part.at[shard, high], xr1.at[d], left),
            )
        )
    seconds = []
    for d, (from_left, from_right) in zip(order, firsts):
        shard = multiply(me.zline(d), me.xs(1))
        from_left.wait_recv()
        part[shard, low, :] += xl1[d]
        one = wire.go(part.at[shard], xl2.at[d], right)
        shard = multiply(me.zline(d), me.xs(3))
        from_right.wait_recv()
        part[shard, high, :] += xr1[d]
        two = wire.go(part.at[shard], xr2.at[d], left)
        seconds.append((one, two))
    for d in order:
        multiply(me.zline(d), me.x)
    arrivals = []
    for d, (from_left, from_right) in zip(order, seconds):
        shard = me.zline(d) * 4 + me.x
        from_left.wait_recv()
        from_right.wait_recv()
        part[shard] += xl2[d] + xr2[d]
        if d:
            arrivals.append(wire.go(part.at[shard], zin.at[d - 1], line[d]))
    for copy in arrivals:
        copy.wait_recv()
    total = part[me.col] + zin[0] + zin[1] + zin[2]

    for i in range(TPB):
        rows = pl.ds(i * TILE, TILE)
        counts = jnp.broadcast_to(total[BLK + i : BLK + i + 1, :], (TILE, TILE)).T
        degree = 1.0 + counts
        pre = selfp[rows, :] + total[i * TILE : (i + 1) * TILE, :] / degree + bias_ref[...]
        sig = jax.nn.sigmoid(pre)
        hid_ref[rows, :] = pre * sig
        grad = cot_ref[rows, :] * sig * (1.0 + pre * (1.0 - sig))
        gp_ref[rows, :] = grad
        sall_ref[me.col, rows, :] = grad / degree

    def spread(block_col):
        return (
            wire.go(sall_ref.at[block_col], sall_ref.at[block_col], right),
            wire.go(sall_ref.at[block_col], sall_ref.at[block_col], left),
        )

    def pass_on(zl, pair):
        pair[0].wait_recv()
        from_left = zl * 4 + me.xs(3)
        one = wire.go(sall_ref.at[from_left, pl.ds(0, HALF)], sall_ref.at[from_left, pl.ds(0, HALF)], right)
        pair[1].wait_recv()
        from_right = zl * 4 + me.xs(1)
        two = wire.go(sall_ref.at[from_right, pl.ds(HALF, HALF)], sall_ref.at[from_right, pl.ds(HALF, HALF)], left)
        return one, two

    sent = {d: wire.go(sall_ref.at[me.col], sall_ref.at[me.col], line[d]) for d in (1, 3, 2)}
    pending = [(me.zl, spread(me.col))]
    gself_ref[...] = dot_f32(feat_ref[...], gp_ref[...], ((0,), (0,)))
    gbias_ref[...] = jnp.sum(gp_ref[...], axis=0, keepdims=True)
    last = []
    for d in (1, 3, 2):
        zl = me.zline(4 - d)
        sent[d].wait_recv()
        pending.append((zl, spread(zl * 4 + me.x)))
        last += pass_on(*pending.pop(0))
    last += pass_on(*pending.pop(0))
    for copy in last:
        copy.wait_recv()
    wire.drain()


def backward_kernel(cols_ref, adjt_ref, scaled_ref, hid_ref, back_ref, hid_out, hid_sem):
    step = pl.program_id(0)
    rows = scaled_ref.shape[0]
    hidden = pltpu.make_async_copy(hid_ref, hid_out, hid_sem.at[0])

    @pl.when(step == 0)
    def _():
        hidden.start()
        back_ref[...] = jnp.zeros_like(back_ref)

    for start in range(0, rows, 4):
        parts = []
        for i in range(start, start + 4):
            both = jnp.dot(adjt_ref[i], split(scaled_ref[i]), preferred_element_type=F32)
            parts.append(both[:, :TILE] + both[:, TILE:])
        for i in range(start, start + 4):
            t = step * rows + i
            back_ref[cols_ref[0, t]] += parts[i - start][:TILE]
            back_ref[cols_ref[1, t]] += parts[i - start][TILE:]

    @pl.when(step == pl.num_programs(0) - 1)
    def _():
        hidden.wait()


SUM_COPIES = 7 + 3 + 7 + 3 + 7
LATE_COPIES = 31 + 7 + 31
BACK_COPIES = 8 + 8 + 4 + SUM_COPIES + LATE_COPIES


def others(me):
    return [(me.core, me.xs(2)), (1 - me.core, me.xs(2))] + [
        (me.core, me.xs(1)), (1 - me.core, me.xs(1)), (me.core, me.xs(3)), (1 - me.core, me.xs(3)), (1 - me.core, me.x)
    ]


def plane(me):
    return [
        (1 - me.core if dc else me.core, me.xs(dx), me.ys(dy))
        for dx in (2, 1, 3, 0)
        for dy in (2, 1, 3, 0)
        for dc in (1, 0)
        if dc or dx or dy
    ]


def pack_rows(pack, rows):
    for n in range(32):
        pack[n // 16, n // 4 % 4, n % 4, pl.ds(0, 8), :] = rows[n * 8 : (n + 1) * 8, :]


def total_over_all(me, wire, pack, r1, r2, r3, full):
    copies = [wire.go(pack.at[c, x], r1.at[n], me.at(core=c, x=x)) for n, (c, x) in enumerate(others(me))]
    yield
    for copy in copies:
        copy.wait_recv()
    total = pack[me.core, me.x] + r1[0]
    for n in range(1, 7):
        total = total + r1[n]
    pack[me.core, me.x] = total
    copies = [wire.go(pack.at[me.core, me.x, me.ys(d)], r2.at[d - 1], me.at(y=me.ys(d))) for d in (2, 1, 3)]
    yield
    for copy in copies:
        copy.wait_recv()
    r3[me.z] = pack[me.core, me.x, me.y] + r2[0] + r2[1] + r2[2]
    copies = [wire.go(r3.at[me.z], r3.at[me.z], me.at(z=me.zs(d))) for d in (4, 3, 5, 2, 6, 1, 7)]
    yield
    for copy in copies:
        copy.wait_recv()
    total = r3[0]
    for n in range(1, 8):
        total = total + r3[n]
    full[me.core, me.x, me.y] = total
    view = full.at[me.core, me.x, me.y]
    copies = [wire.go(view, view, me.at(y=me.ys(d))) for d in (2, 1, 3)]
    yield
    for copy in copies:
        copy.wait_recv()
    view = full.at[me.core, me.x]
    copies = [wire.go(view, view, me.at(core=c, x=x)) for c, x in others(me)]
    yield
    for copy in copies:
        copy.wait_recv()
    yield


def total_by_planes(me, wire, pack, r1, r3, full):
    copies = [wire.go(pack.at[c, x, y], r1.at[n], me.at(core=c, x=x, y=y)) for n, (c, x, y) in enumerate(plane(me))]
    yield
    for copy in copies:
        copy.wait_recv()
    total = pack[me.core, me.x, me.y]
    for n in range(31):
        total = total + r1[n]
    r3[me.z] = total
    copies = [wire.go(r3.at[me.z], r3.at[me.z], me.at(z=me.zs(d))) for d in (4, 3, 5, 2, 6, 1, 7)]
    yield
    for copy in copies:
        copy.wait_recv()
    total = r3[0]
    for n in range(1, 8):
        total = total + r3[n]
    full[me.core, me.x, me.y] = total
    view = full.at[me.core, me.x, me.y]
    copies = [wire.go(view, view, me.at(core=c, x=x, y=y)) for c, x, y in plane(me)]
    yield
    for copy in copies:
        copy.wait_recv()
    yield


def return_kernel(
    back_ref, feat_ref, gp_ref, ws_ref, wn_ref, gself_ref, gbias_ref,
    gf_ref, gs_ref, gn_ref,
    sums, rc, yl1, yr1, yl2, yr2, zin, zrel, pack_s, a1, a2, a3, pack_n, b1, b3, send, recv,
):
    me = Place()
    wire = Wire(send, recv)
    up, down = me.at(y=me.ys(1)), me.at(y=me.ys(3))
    far, near = me.at(z=me.zs(2)), me.at(z=me.zs(6))
    partner = me.partner()
    peers = [me.at(core=c, x=x, y=y) for c, x, y in plane(me)]
    peers += [me.at(z=me.zs(d)) for d in range(1, 8)]
    barrier = greet(peers)
    other = 1 - me.zh
    order = [(other, 2), (me.zh, 2), (other, 1), (other, 3), (me.zh, 1), (me.zh, 3), (other, 0), (me.zh, 0)]

    def group(zh, d):
        return zh * 4 + me.ys(d)

    pack_rows(pack_s, gself_ref[...])
    pack_s[:, :, :, pl.ds(8, 8), :] = jnp.zeros((2, 4, 4, 8, TILE), F32)
    pack_s[0, 0, 0, pl.ds(8, 1), :] = gbias_ref[...]
    pl.semaphore_wait(barrier, len(peers))

    early = total_over_all(me, wire, pack_s, a1, a2, a3, gs_ref)
    next(early)
    from_core = {}
    for n, (zh, d) in enumerate(order):
        g = group(zh, d)
        from_core[n] = wire.go(back_ref.at[g, 1 - me.core], rc.at[g], partner)

    gf_ref[...] = dot_f32(gp_ref[...], ws_ref[...], ((1,), (1,)))

    def summed(n):
        zh, d = order[n]
        g = group(zh, d)
        from_core[n].wait_recv()
        sums[g] = back_ref[g, me.core] + rc[g]
        return g

    low, high = pl.ds(0, HALF), pl.ds(HALF, HALF)
    firsts = []
    for n in (0, 1):
        g = summed(n)
        firsts.append((wire.go(sums.at[g, low], yl1.at[n], up), wire.go(sums.at[g, high], yr1.at[n], down)))
    seconds = []
    for n in (0, 1):
        g = summed(2 + 2 * n)
        firsts[n][0].wait_recv()
        sums[g, low, :] += yl1[n]
        one = wire.go(sums.at[g], yl2.at[n], up)
        g = summed(3 + 2 * n)
        firsts[n][1].wait_recv()
        sums[g, high, :] += yr1[n]
        two = wire.go(sums.at[g], yr2.at[n], down)
        seconds.append((one, two))
        next(early)

    def finished(n):
        g = summed(6 + n)
        seconds[n][0].wait_recv()
        seconds[n][1].wait_recv()
        sums[g] += yl2[n] + yr2[n]
        return g

    g = finished(0)
    z_up = wire.go(sums.at[g, low], zrel.at[0], far)
    z_down = wire.go(sums.at[g, high], zrel.at[1], near)
    next(early)
    z_up.wait_recv()
    zf_up = wire.go(zrel.at[0], zin.at[low], far)
    z_down.wait_recv()
    zf_down = wire.go(zrel.at[1], zin.at[high], near)
    next(early)
    g = finished(1)
    zf_up.wait_recv()
    zf_down.wait_recv()
    back_rows = sums[g] + zin[...]

    pack_rows(pack_n, dot_f32(feat_ref[...], back_rows, ((0,), (0,))))
    late = total_by_planes(me, wire, pack_n, b1, b3, gn_ref)
    next(late)
    gf_ref[...] += dot_f32(back_rows, wn_ref[...], ((1,), (1,)))
    next(early)
    for _ in range(3):
        next(late)
    wire.drain()


def finish_kernel(factor, gf_ref, gs_ref, gn_ref, gf_out, gs_out, gn_out, gb_out, sem):
    copy = pltpu.make_async_copy(gf_ref, gf_out, sem.at[0])
    copy.start()
    for n in range(32):
        place = (n // 16, n // 4 % 4, n % 4)
        gs_out[pl.ds(n * 8, 8), :] = gs_ref[place][:8] * factor
        gn_out[pl.ds(n * 8, 8), :] = gn_ref[place] * factor
    gb_out[...] = gs_ref[0, 0, 0, pl.ds(8, 1), :] * factor
    copy.wait()


def local(features, self_weight, neigh_weight, out_bias, adjacency_tiles, tile_columns, live_counts, cotangent):
    vmem = pl.BlockSpec(memory_space=pltpu.VMEM)
    smem = pl.BlockSpec(memory_space=pltpu.SMEM)
    hbm = pl.BlockSpec(memory_space=pltpu.HBM)
    fin, fout = self_weight.shape

    def shape(*dims, dtype=F32):
        return jax.ShapeDtypeStruct(dims, dtype)

    dma = pltpu.SemaphoreType.DMA
    cols = tile_columns.T
    hidden, grad_pre, scaled, adjt, gself, gbias, feat, ws, wn = pl.pallas_call(
        forward_kernel,
        out_shape=[
            shape(BLK, fout),
            shape(BLK, fout),
            shape(GRID, BLK, fout),
            shape(TROWS, 2 * TILE, TILE, dtype=BF16),
            shape(fin, fout),
            shape(1, fout),
            shape(BLK, fin),
            shape(fin, fout),
            shape(fin, fout),
        ],
        in_specs=[hbm] * 8,
        out_specs=[vmem] * 9,
        scratch_shapes=[
            pltpu.VMEM((TROWS, TILE, fout), F32),
            pltpu.VMEM((TROWS, TILE, 2 * TILE), BF16),
            pltpu.VMEM((GRID, BLK + DEG, fout), F32),
            pltpu.VMEM((4, HALF, fout), F32),
            pltpu.VMEM((4, HALF + DEG, fout), F32),
            pltpu.VMEM((4, BLK + DEG, fout), F32),
            pltpu.VMEM((4, BLK + DEG, fout), F32),
            pltpu.VMEM((3, BLK + DEG, fout), F32),
            pltpu.VMEM((2, TPB // 2, TILE, fout), F32),
            pltpu.VMEM((BLK, fout), F32),
            pltpu.VMEM((2, TPB, 2, TILE, TILE), jnp.int32),
            pltpu.VMEM((1, fout), F32),
            pltpu.VMEM((BLK, fout), F32),
            pltpu.SMEM((2, TROWS), jnp.int32),
            pltpu.SMEM((1, TROWS), jnp.int32),
            dma((2,)),
            dma((7,)),
            dma((FWD_COPIES,)),
            dma((FWD_COPIES,)),
        ],
        compiler_params=pltpu.CompilerParams(collective_id=0, has_side_effects=True, vmem_limit_bytes=24 << 20),
        name="forward",
    )(
        *(
            pltpu.with_memory_space_constraint(given, pltpu.HBM)
            for given in (
                cols,
                live_counts.T,
                features,
                self_weight,
                neigh_weight,
                out_bias.reshape(1, fout),
                cotangent,
                adjacency_tiles,
            )
        ),
    )

    steps = 8
    rows = TROWS // steps
    back, hidden = pl.pallas_call(
        backward_kernel,
        grid=(steps,),
        out_shape=[shape(TROWS, TILE, fout), shape(BLK, fout)],
        in_specs=[
            smem,
            pl.BlockSpec((rows, 2 * TILE, TILE), lambda i: (i, 0, 0)),
            pl.BlockSpec((rows, TILE, fout), lambda i: (i, 0, 0)),
            pl.BlockSpec(memory_space=pl.ANY),
        ],
        out_specs=[pl.BlockSpec((TROWS, TILE, fout), lambda i: (0, 0, 0)), pl.BlockSpec(memory_space=pltpu.HBM)],
        scratch_shapes=[dma((1,))],
        compiler_params=pltpu.CompilerParams(vmem_limit_bytes=16 << 20),
        name="backward",
    )(cols, adjt, scaled.reshape(TROWS, TILE, fout), hidden)

    grad_features, total_self, total_neigh = pl.pallas_call(
        return_kernel,
        out_shape=[shape(BLK, fin), shape(2, 4, 4, 16, fout), shape(2, 4, 4, 8, fout)],
        in_specs=[vmem] * 7,
        out_specs=[vmem] * 3,
        scratch_shapes=[
            pltpu.VMEM((8, BLK, fout), F32),
            pltpu.VMEM((8, BLK, fout), F32),
            pltpu.VMEM((2, HALF, fout), F32),
            pltpu.VMEM((2, HALF, fout), F32),
            pltpu.VMEM((2, BLK, fout), F32),
            pltpu.VMEM((2, BLK, fout), F32),
            pltpu.VMEM((BLK, fout), F32),
            pltpu.VMEM((2, HALF, fout), F32),
            pltpu.VMEM((2, 4, 4, 16, fout), F32),
            pltpu.VMEM((7, 4, 16, fout), F32),
            pltpu.VMEM((3, 16, fout), F32),
            pltpu.VMEM((8, 16, fout), F32),
            pltpu.VMEM((2, 4, 4, 8, fout), F32),
            pltpu.VMEM((31, 8, fout), F32),
            pltpu.VMEM((8, 8, fout), F32),
            dma((BACK_COPIES,)),
            dma((BACK_COPIES,)),
        ],
        compiler_params=pltpu.CompilerParams(collective_id=1, has_side_effects=True, vmem_limit_bytes=24 << 20),
        name="backward_return",
    )(back.reshape(8, 2, BLK, fout), feat, grad_pre, ws, wn, gself, gbias)

    nodes = BLK * lax.axis_size("row") * lax.axis_size("col")
    factor = 1.0 / math.sqrt(nodes)
    grad_features, grad_self, grad_neigh, grad_bias = pl.pallas_call(
        lambda *refs: finish_kernel(factor, *refs),
        out_shape=[shape(BLK, fin), shape(fin, fout), shape(fin, fout), shape(1, fout)],
        in_specs=[pl.BlockSpec(memory_space=pl.ANY), vmem, vmem],
        out_specs=[pl.BlockSpec(memory_space=pltpu.HBM), vmem, vmem, vmem],
        scratch_shapes=[dma((1,))],
        compiler_params=pltpu.CompilerParams(vmem_limit_bytes=8 << 20),
        name="finish",
    )(grad_features, total_self, total_neigh)
    return hidden, grad_features, grad_self, grad_neigh, grad_bias.reshape(fout)


def solution(mesh):
    return jax.shard_map(
        local,
        mesh=mesh,
        in_specs=(
            P(("row", "col"), None),
            P(),
            P(),
            P(),
            P("row", "col", None, None),
            P("row", "col"),
            P("row", "col"),
            P(("row", "col"), None),
        ),
        out_specs=(P(("row", "col"), None), P(("row", "col"), None), P(), P(), P()),
        check_vma=False,
    )
```
